32 devices in a mesh: groups: 2 (over y), lon: 4 (over z), lat: 2 (over x), dp: 2 (over core).
Axes of the slice: x: 2, y: 2, z: 4, core: 2. Of those that a mesh axis runs over, the one named last changes fastest.
Arguments:
- inputs: bfloat16 [4, 128, 1024, 128], P(('groups', 'dp'), 'lat', 'lon'), parts along dimension 0, may hold values from -6 to 6
- cotangent: bfloat16 [4, 128, 1024, 128], P(('groups', 'dp'), 'lat', 'lon'), parts along dimension 0, may hold values from -6 to 6
- kernel_dw: bfloat16 [7, 7, 128], replicated, may hold values from -0.875 to 0.875
- bias_dw: float32 [128], replicated, may hold values from -3 to 3
- gain: float32 [128], replicated, may hold values from 0.1 to 1.9
- shift_ln: float32 [128], replicated, may hold values from -2 to 2
- w_in: bfloat16 [128, 256], replicated, may hold values from -0.5 to 0.5
- b_in: float32 [256], replicated, may hold values from -2 to 2
- w_out: bfloat16 [256, 128], replicated, may hold values from -0.375 to 0.375
- ocean_mask: int32 [2, 16], P('lat', 'lon'), may hold values from 0 to 1, as said below
Outputs:
- grad_inputs: bfloat16 [4, 128, 1024, 128], P(('groups', 'dp'), 'lat', 'lon'), parts along dimension 0
- grad_w_in: float32 [256, 256], P(('groups', 'dp')), parts along dimension 0
- grad_w_out: float32 [512, 128], P(('groups', 'dp')), parts along dimension 0
- grad_kernel: float32 [14, 7, 128], P('groups'), parts along dimension 0
- grad_bias_dw: float32 [256], P('groups'), parts along dimension 0
- grad_gain: float32 [256], P('groups'), parts along dimension 0
- grad_shift: float32 [256], P('groups'), parts along dimension 0
- grad_b_in: float32 [512], P('groups'), parts along dimension 0
The draws below stay inside these ranges and needn't reach their ends.
There are 2 independent parts, one for each index of `groups`. The reference program is written for one: setup_inputs(seed, part) draws one part's arguments, and reference() takes and returns one part's arrays. A program takes and returns all parts, laid end to end along the dimension named above; an argument that names none is the same for every part. Nothing has to cross between parts.
Inputs may be any that keep to these rules, and one draw needn't show every extreme that they name: `ocean_mask`: every block of the northernmost block row (index 1) is ocean, and each aligned run of 4 blocks of a block row holds at least one ocean block.
All inputs are finite; a program needn't handle non-finite values.
Results may differ from the reference program's by a relative error of at most 0.0056.
Values may be sent and summed in bfloat16 or wider, within the bound.
A program may use at most 128 MiB of HBM per device.

```python
import math
import jax
import jax.numpy as jnp
from jax import lax

BLK = 64
BLOCKS_DEV = 4
C = 128
HID = 256
KS = 7
BATCH = 2
H = 128
W = 1024
HB = 2
WB = 16


def draw_ocean_mask(key, part):
    key_shift, key_roll, key_pick = jax.random.split(jax.random.fold_in(key, 17), 3)
    columns = jnp.arange(WB, dtype=jnp.int32)
    offset = jax.random.randint(key_shift, (), 0, WB, dtype=jnp.int32)
    wave = (columns + offset) % WB
    triangle = jnp.minimum(wave, WB - wave)
    limit = 10 + 160 * triangle // WB
    rolled = jax.random.randint(key_roll, (HB, WB), 0, 100, dtype=jnp.int32)
    ocean = rolled < limit[None, :]
    picked = jax.random.randint(key_pick, (HB, WB // BLOCKS_DEV), 0, BLOCKS_DEV, dtype=jnp.int32)
    forced = (columns % BLOCKS_DEV)[None, :] == jnp.repeat(picked, BLOCKS_DEV, axis=1)
    northern = (jnp.arange(HB, dtype=jnp.int32) == HB - 1)[:, None]
    return jnp.where(forced | northern | ocean, 1, 0).astype(jnp.int32)


def steps_of(stream_key, shape, cuts, smallest, top_value):
    loudness, own = 1.0, jax.random.fold_in(stream_key, 6)
    for axis_at, blocks in cuts:
        draws = jnp.exp(jax.random.uniform(jax.random.fold_in(own, axis_at), (blocks,), jnp.float32, smallest / len(cuts), top_value / len(cuts)))
        loudness = loudness * jnp.repeat(draws, shape[axis_at] // blocks).reshape([-1 if axis == axis_at else 1 for axis in range(len(shape))])
    return loudness


def normal_values(rng, shape, deviation, reach, shards=(), held_as=jnp.bfloat16):
    drawn = deviation * jax.random.normal(rng, shape, jnp.float32)
    if shards:
        drawn = drawn * steps_of(rng, shape, shards, -0.22, 0.18)
    return jnp.clip(drawn, -reach, reach).astype(held_as)


def setup_inputs(seed: int = 0, part: int = 0) -> dict:
    seeds = jax.random.split(jax.random.key(seed), 11)
    own_keys = jax.random.split(jax.random.fold_in(seeds[10], part), 11)
    return {
        "inputs": normal_values(own_keys[0], (BATCH, H, W, C), 1.0, 6.0, ((0, 2), (1, 2), (2, 4))),
        "cotangent": normal_values(own_keys[1], (BATCH, H, W, C), 1.0, 6.0, ((0, 2), (1, 2), (2, 4))),
        "kernel_dw": normal_values(seeds[2], (KS, KS, C), (KS * KS) ** -0.5, 0.875),
        "bias_dw": normal_values(seeds[3], (C,), 0.5, 3.0, (), jnp.float32),
        "gain": jnp.clip(1.0 + 0.18 * jax.random.normal(seeds[4], (C,), jnp.float32), 0.1, 1.9),
        "shift_ln": normal_values(seeds[5], (C,), 0.3, 2.0, (), jnp.float32),
        "w_in": normal_values(seeds[6], (C, HID), C ** -0.5, 0.5),
        "b_in": normal_values(seeds[7], (HID,), 0.3, 2.0, (), jnp.float32),
        "w_out": normal_values(seeds[8], (HID, C), HID ** -0.5, 0.375),
        "ocean_mask": draw_ocean_mask(jax.random.fold_in(seeds[10], 71), part),
    }


EPS = 1e-06
GELU_K = 0.7978845608
GELU_C = 0.044715

def extend(field):
    half = KS // 2
    height = field.shape[0]
    south = jnp.zeros((half,) + field.shape[1:], field.dtype)
    north = field[height - half:][::-1, ::-1, :]
    framed = jnp.concatenate([south, field, north], 0)
    width = field.shape[1]
    return jnp.concatenate([framed[:, width - half:], framed, framed[:, :half]], 1)

def conv_valid(extended, kernel):
    return lax.conv_general_dilated(extended, kernel[:, :, None, :], (1, 1), 'VALID', dimension_numbers=('NHWC', 'HWIO', 'NHWC'), feature_group_count=extended.shape[3], preferred_element_type=jnp.float32)

def kernel_grad(extended, delta):
    out = lax.conv_general_dilated(extended[None], delta[:, :, None, :], (1, 1), 'VALID', dimension_numbers=('NHWC', 'HWIO', 'NHWC'), feature_group_count=extended.shape[2], preferred_element_type=jnp.float32)
    return out[0]

def cell_grads(ycells, gcells, maskval, gain, shift_ln, w_in, b_in, w_out):
    center = ycells - lax.optimization_barrier(jnp.mean(ycells, -1, keepdims=True))
    rstd = lax.rsqrt(lax.optimization_barrier(jnp.mean(center * center, -1, keepdims=True)) + EPS)
    nhat = center * rstd
    normed = (nhat * gain + shift_ln).astype(jnp.bfloat16)
    pre = jnp.dot(normed, w_in, preferred_element_type=jnp.float32) + b_in
    tangent = jnp.tanh(GELU_K * (pre + GELU_C * pre * pre * pre))
    act = (0.5 * pre * (1.0 + tangent)).astype(jnp.bfloat16)
    outgrad = (gcells.astype(jnp.float32) * maskval).astype(jnp.bfloat16)
    g_out = lax.dot_general(act, outgrad, (((0,), (0,)), ((), ())), preferred_element_type=jnp.float32)
    dact = lax.dot_general(outgrad, w_out, (((1,), (1,)), ((), ())), preferred_element_type=jnp.float32)
    slope = 0.5 * (1.0 + tangent) + 0.5 * pre * (1.0 - tangent * tangent) * GELU_K * (1.0 + 3.0 * GELU_C * pre * pre)
    dpre = dact * slope
    dpre_b = dpre.astype(jnp.bfloat16)
    g_in = lax.dot_general(normed, dpre_b, (((0,), (0,)), ((), ())), preferred_element_type=jnp.float32)
    g_bin = lax.optimization_barrier(jnp.sum(dpre, 0))
    dnorm = lax.dot_general(dpre_b, w_in, (((1,), (1,)), ((), ())), preferred_element_type=jnp.float32)
    g_gain = lax.optimization_barrier(jnp.sum(dnorm * nhat, 0))
    g_shift = lax.optimization_barrier(jnp.sum(dnorm, 0))
    dscaled = dnorm * gain
    delta = rstd * (dscaled - lax.optimization_barrier(jnp.mean(dscaled, -1, keepdims=True)) - nhat * lax.optimization_barrier(jnp.mean(dscaled * nhat, -1, keepdims=True)))
    return (delta.astype(jnp.bfloat16), (g_in, g_bin, g_out, g_gain, g_shift))

def to_blocks(field):
    height, width, chans = field.shape
    parts = field.reshape(height // BLK, BLK, width // BLK, BLK, chans).transpose(0, 2, 1, 3, 4)
    return parts.reshape(-1, BLK * BLK, chans)

def from_blocks(parts, height, width):
    chans = parts.shape[-1]
    grid = parts.reshape(height // BLK, width // BLK, BLK, BLK, chans).transpose(0, 2, 1, 3, 4)
    return grid.reshape(height, width, chans)

def reference(inputs, cotangent, kernel_dw, bias_dw, gain, shift_ln, w_in, b_in, w_out, ocean_mask):
    batch, height, width, chans = inputs.shape
    hidden = w_in.shape[1]
    half = KS // 2
    flat_mask = ocean_mask.reshape(-1).astype(jnp.float32)
    totals = (jnp.zeros((chans, hidden), jnp.float32), jnp.zeros((hidden,), jnp.float32), jnp.zeros((hidden, chans), jnp.float32), jnp.zeros((chans,), jnp.float32), jnp.zeros((chans,), jnp.float32))
    g_kernel = jnp.zeros((KS, KS, chans), jnp.float32)
    g_bias = jnp.zeros((chans,), jnp.float32)

    def step(carry, items):
        ycells, gcells, maskval = items
        delta, grads = cell_grads(ycells, gcells, maskval, gain, shift_ln, w_in, b_in, w_out)
        return (tuple((c + g for c, g in zip(carry, grads))), delta)
    results = []
    for sample in range(batch):
        extended = extend(inputs[sample])
        field_y = conv_valid(extended[None], kernel_dw)[0] + bias_dw
        totals, deltas = lax.scan(step, totals, (to_blocks(field_y), to_blocks(cotangent[sample]), flat_mask))
        delta = from_blocks(deltas, height, width)
        g_kernel = g_kernel + kernel_grad(extended, delta)
        g_bias = g_bias + lax.optimization_barrier(jnp.sum(delta.astype(jnp.float32), (0, 1)))
        spread = extend(delta)
        direct_part = spread.at[height + half:].set(jnp.zeros_like(spread[height + half:]))
        direct = conv_valid(direct_part[None], kernel_dw[::-1, ::-1])[0]
        fold_part = jnp.concatenate([jnp.zeros_like(spread[height - half:height + half]), spread[height + half:]], 0)
        fold = conv_valid(fold_part[None], kernel_dw)[0]
        total = cotangent[sample].astype(jnp.float32) + direct
        total = total.at[height - half:].add(fold)
        results.append(total.astype(jnp.bfloat16))
    scale = 1.0 / math.sqrt(batch * height * width)
    g_in, g_bin, g_out, g_gain, g_shift = totals
    return (jnp.stack(results), g_in * scale, g_out * scale, g_kernel * scale, g_bias * scale, g_gain * scale, g_shift * scale, g_bin * scale)
```

```python
import math

import jax
import jax.numpy as jnp
import numpy as np
from jax import lax
from jax.experimental import pallas as pl
from jax.experimental.pallas import tpu as pltpu
from jax.sharding import PartitionSpec as P

KS = 7
HALF = 3
EPS = 1e-06
GELU_K = 0.7978845608
GELU_C = 0.044715
F32 = jnp.float32
BF16 = jnp.bfloat16
TR = 8
TC = 16
LANES = TR * TC
CHUNKS = TC // 8 + 1
DEPTH = CHUNKS * LANES
OFF = 8
NT = (((1,), (1,)), ((), ()))
TN = (((0,), (0,)), ((), ()))


def spread():
    jb, ri, ji, ro, jo = np.meshgrid(*(np.arange(n) for n in (CHUNKS, 2, 8, TR, TC)), indexing="ij")
    a = (ri - ro) % 8
    b = 8 * jb + ji - jo - 1
    tap = np.where((a < KS) & (b >= 0) & (b < KS), a * KS + b, -1)
    hot = tap.reshape(1, -1) == np.arange(KS * KS)[:, None]
    return hot.astype(np.float32)


def row_masks():
    p, ri, ji, ro, jo = np.meshgrid(*(np.arange(n) for n in (4, 2, 8, TR, TC)), indexing="ij")
    low = (ro <= 2 * p + ri).reshape(4, 1, 16, LANES)
    both = np.concatenate([low, ~low], 0).astype(np.float32)
    return np.broadcast_to(both, (8, CHUNKS, 16, LANES)).reshape(8 * CHUNKS * 16, LANES)


def gather_taps():
    s, jb, ri, ji = np.meshgrid(*(np.arange(n) for n in (8, 2, 16, 8)), indexing="ij")
    b = 8 * jb + ji - s - 1
    tap = np.where((ri < KS) & (b >= 0) & (b < KS), ri * KS + b, -1)
    return (tap.reshape(-1, 1) == np.arange(LANES)[None]).astype(np.float32)


def load_extended(ext, tile, south, north, west, east):
    rows, cols, chans = tile.shape

    def fill(r, carry):
        ext[r + HALF, OFF : OFF + cols, :] = tile[r].astype(F32)
        return carry

    lax.fori_loop(0, rows, fill, 0, unroll=2)
    for m in range(HALF):
        ext[m, OFF : OFF + cols, :] = south[m].astype(F32)
        ext[rows + HALF + m, OFF : OFF + cols, :] = north[m].astype(F32)
    for m in range(rows + 2 * HALF, ext.shape[0]):
        ext[m] = jnp.zeros(ext.shape[1:], F32)
    blank = jnp.zeros((OFF, chans), F32)

    def sides(r, carry):
        ext[r, :OFF, :] = blank
        ext[r, OFF + cols :, :] = blank
        ext[r, OFF - HALF : OFF, :] = west[r].astype(F32)
        ext[r, OFF + cols : OFF + cols + HALF, :] = east[r].astype(F32)
        return carry

    lax.fori_loop(0, rows + 2 * HALF, sides, 0)


def make_patches(ext, patches, rows, cols):
    bands = rows // TR
    chans = ext.shape[-1]
    step = bands + 1

    def piece(jc):
        at = pl.multiple_of(jc * 8, 8) + (OFF - 4)
        for q in range(bands):
            block = jnp.concatenate([ext[q * TR + k, pl.ds(at, 8), :] for k in range(2 * TR)], 0)
            turned = block.astype(BF16).T.astype(F32)
            patches[pl.ds(jc * (chans * step) + q, chans, stride=step), :] = turned

    def pieces(jc, carry):
        piece(jc)
        return carry

    lax.fori_loop(0, cols // 8, pieces, 0, unroll=4)
    piece(cols // 8)


def patch_rows(patches, c, chans, bands, across):
    step = bands + 1

    def block(jc):
        return patches[pl.ds(jc * (chans * step) + c * step, bands), :]

    parts = []
    for jb in range(CHUNKS):
        parts.append(jnp.concatenate([block(2 * u + jb) for u in range(across)], 0).astype(BF16))
    return jnp.concatenate(parts, 1)


def conv_patches(patches, master, masks, y, chans, bands, across, pitch):
    width = CHUNKS * 16

    def channel(c, carry):
        base = master[pl.ds(pl.multiple_of(c * width, width), width), :]
        turned = [base] + [pltpu.roll(base, 32 * s, 1) for s in range(1, 4)]
        strips = [turned[p % 4] * masks[p * width : (p + 1) * width, :] for p in range(8)]
        weights = jnp.concatenate(
            [strips[p][16 * jb : 16 * jb + 16] for jb in range(CHUNKS) for p in range(8)], 0
        )
        rows = patch_rows(patches, c, chans, bands, across)
        y[pl.ds(pl.multiple_of(c * pitch, 8), bands * across), :] = jnp.dot(
            rows, weights, preferred_element_type=F32
        )
        return carry

    lax.fori_loop(0, chans, channel, 0, unroll=16)


def cells_kernel(
    blocks, tile, south, north, west, east, cot, master, masks, bias, gain, shift, w_in_t, b_in, w_out, w_in,
    gather,
    dy, g_in, g_out, g_chan, g_bin, g_taps,
    ext, patches, y, s_chan, s_bin, s_taps,
):
    rows, cols, chans = tile.shape
    hidden = w_out.shape[0]
    bands, across = rows // TR, cols // TC
    tiles = bands * across
    pitch = tiles + 8
    per_block = across // blocks.shape[0]
    load_extended(ext, tile, south, north, west, east)
    make_patches(ext, patches, rows, cols)
    conv_patches(patches, master, masks, y, chans, bands, across, pitch)
    g_in[...] = jnp.zeros_like(g_in)
    g_out[...] = jnp.zeros_like(g_out)
    s_chan[...] = jnp.zeros_like(s_chan)
    s_bin[...] = jnp.zeros_like(s_bin)
    inv = 1.0 / chans

    def wide(x):
        return jnp.concatenate([x, x], 1)

    def half_sum(x):
        return x[:, :LANES] + x[:, LANES:]

    def step(i, carry):
        u = i // (bands // 2)
        q = (i % (bands // 2)) * 2
        t = u * bands + q
        yc = jnp.concatenate([y[pl.ds(t + k, chans, stride=pitch), :] for k in range(2)], 1) + wide(bias[...])
        center = yc - jnp.sum(yc, 0, keepdims=True) * inv
        rstd = lax.rsqrt(jnp.sum(center * center, 0, keepdims=True) * inv + EPS)
        nhat = center * rstd
        scale = wide(gain[...])
        normed = (nhat * scale + wide(shift[...])).astype(BF16)
        pre = jnp.dot(w_in_t[...], normed, preferred_element_type=F32) + wide(b_in[...])
        square = pre * pre
        th = jnp.tanh(pre * (GELU_K + (GELU_K * GELU_C) * square))
        h = 0.5 + 0.5 * th
        act = pre * h
        slope = h + act * (1.0 - h) * (2.0 * GELU_K + (6.0 * GELU_K * GELU_C) * square)
        sea = blocks[u // per_block].astype(F32).astype(BF16)
        at = pl.ds(pl.multiple_of(u * TC, TC), TC)
        og = cot[pl.ds(q * TR, 2 * TR), at, :].reshape(2 * LANES, chans) * sea
        g_out[...] += jnp.dot(act.astype(BF16), og, preferred_element_type=F32)
        dact = lax.dot_general(w_out[...], og, NT, preferred_element_type=F32)
        dpre = dact * slope
        dpre_b = dpre.astype(BF16)
        s_bin[...] += half_sum(dpre)
        g_in[...] += lax.dot_general(normed, dpre_b, NT, preferred_element_type=F32)
        dnorm = jnp.dot(w_in[...], dpre_b, preferred_element_type=F32)
        s_chan[0] += half_sum(dnorm * nhat)
        s_chan[1] += half_sum(dnorm)
        dn = dnorm * scale
        m1 = jnp.sum(dn, 0, keepdims=True) * inv
        m2 = jnp.sum(dn * nhat, 0, keepdims=True) * inv
        delta = (rstd * (dn - m1 - nhat * m2)).astype(BF16).astype(F32)
        s_chan[2] += half_sum(delta)
        for k in range(2):
            part = delta[:, k * LANES : (k + 1) * LANES]
            y[pl.ds(t + k, chans, stride=pitch), :] = part
            dy[pl.ds((q + k) * TR, TR), at, :] = part.T.astype(BF16).reshape(TR, TC, chans)
        return carry

    lax.fori_loop(0, tiles // 2, step, 0)
    for n in range(3):
        g_chan[:, n : n + 1] = jnp.sum(s_chan[n], axis=1, keepdims=True)
    g_bin[...] = jnp.sum(s_bin[...], axis=1, keepdims=True)

    def channel(c, carry):
        delta = y[pl.ds(pl.multiple_of(c * pitch, 8), tiles), :].astype(BF16)
        found = lax.dot_general(
            delta, patch_rows(patches, c, chans, bands, across), TN, preferred_element_type=F32
        )
        for jb in range(2):
            acc = None
            for ro in range(TR):
                term = None
                for h in range(TC // 8):
                    at = ro * TC + 8 * h
                    piece = found[at : at + 8, (jb + h) * LANES : (jb + h + 1) * LANES]
                    term = piece if term is None else term + piece
                term = pltpu.roll(term, (LANES - 8 * ro) % LANES, 1) if ro else term
                acc = term if acc is None else acc + term
            s_taps[jb, pl.ds(pl.multiple_of(c * 8, 8), 8), :] = acc
        return carry

    lax.fori_loop(0, chans, channel, 0, unroll=16)
    total = None
    for s in range(8):
        for jb in range(2):
            term = jnp.dot(
                s_taps[jb, pl.ds(s, chans, stride=8), :],
                gather[(2 * s + jb) * LANES : (2 * s + jb + 1) * LANES, :],
                precision=lax.Precision.HIGHEST,
                preferred_element_type=F32,
            )
            total = term if total is None else total + term
    g_taps[...] = total.T


def input_kernel(
    tile, south, north, west, east, cot, master, masks, taps, is_north,
    out,
    ext, patches, y, fold, folded,
):
    rows, cols, chans = tile.shape
    bands, across = rows // TR, cols // TC
    tiles = bands * across
    pitch = tiles + 8
    load_extended(ext, tile, south, north, west, east)
    flag = is_north[0]
    for m in range(HALF):
        row = ext[rows + HALF + m]
        fold[m] = row * flag
        ext[rows + HALF + m] = row * (1.0 - flag)

    def fold_step(i, carry):
        c0 = pl.multiple_of(i * TC, TC)
        for m in range(HALF):
            acc = jnp.zeros((TC // 8, 8, chans), F32)
            for n in range(m + 1):
                a = KS - 1 - m + n
                for b in range(KS):
                    v = fold[n, pl.ds(c0 + (OFF - HALF + b), TC), :]
                    acc = acc + v.reshape(TC // 8, 8, chans) * taps[a * KS + b][None]
            folded[m, pl.ds(c0, TC), :] = acc.reshape(TC, chans)
        return carry

    lax.fori_loop(0, cols // TC, fold_step, 0)
    make_patches(ext, patches, rows, cols)
    conv_patches(patches, master, masks, y, chans, bands, across, pitch)

    def step(u, carry):
        at = pl.ds(pl.multiple_of(u * TC, TC), TC)
        for q in range(bands):
            direct = y[pl.ds(u * bands + q, chans, stride=pitch), :].T.reshape(TR, TC, chans)
            total = direct + cot[q * TR : (q + 1) * TR, at, :].astype(F32)
            if q == bands - 1:
                out[q * TR : rows - HALF, at, :] = total[: TR - HALF].astype(BF16)
                out[rows - HALF : rows, at, :] = (total[TR - HALF :] + folded[:, at, :]).astype(BF16)
            else:
                out[q * TR : (q + 1) * TR, at, :] = total.astype(BF16)
        return carry

    lax.fori_loop(0, across, step, 0)


def row_halo(tile):
    rows = tile.shape[0]
    lats, lons = lax.axis_size("lat"), lax.axis_size("lon")
    low, high = tile[:HALF], tile[rows - HALF :]
    lat = lax.axis_index("lat")
    if lats % 2:
        south = lax.ppermute(high, "lat", [(i, i + 1) for i in range(lats - 1)])
        above = lax.ppermute(low, "lat", [(i + 1, i) for i in range(lats - 1)])
        mirror = lax.ppermute(high, "lon", [(i, lons - 1 - i) for i in range(lons)])
        north = jnp.where(lat == lats - 1, mirror[::-1, ::-1, :], above)
    else:
        odd = lat % 2 == 1
        first = lax.ppermute(jnp.where(odd, low, high), "lat", [(i, i ^ 1) for i in range(lats)])
        route = []
        for j in range(lons):
            mirrored = lons - 1 - j
            route.append((j * lats + lats - 1, mirrored * lats + lats - 1))
            for i in range(1, lats - 1, 2):
                route.append((j * lats + i, j * lats + i + 1))
                route.append((j * lats + i + 1, j * lats + i))
        second = lax.ppermute(jnp.where(odd, high, low), ("lon", "lat"), route)
        folded = jnp.where(lat == lats - 1, second[::-1, ::-1, :], second)
        south = jnp.where(odd, first, second)
        north = jnp.where(odd, folded, first)
    return south, north


def column_halo(tile, south, north):
    cols, lons = tile.shape[1], lax.axis_size("lon")
    left = jnp.concatenate([south[:, :HALF], tile[:, :HALF], north[:, :HALF]], 0)
    right = jnp.concatenate([south[:, cols - HALF :], tile[:, cols - HALF :], north[:, cols - HALF :]], 0)
    west = lax.ppermute(right, "lon", [(i, (i + 1) % lons) for i in range(lons)])
    east = lax.ppermute(left, "lon", [((i + 1) % lons, i) for i in range(lons)])
    return west, east


def call(kernel, out_shape, scratch, flops, *args, scalars=()):
    vmem = pl.BlockSpec(memory_space=pltpu.VMEM)
    smem = pl.BlockSpec(memory_space=pltpu.SMEM)
    return pl.pallas_call(
        kernel,
        out_shape=out_shape,
        in_specs=[smem if n in scalars else vmem for n in range(len(args))],
        out_specs=jax.tree.map(lambda _: vmem, out_shape),
        scratch_shapes=scratch,
        compiler_params=pltpu.CompilerParams(vmem_limit_bytes=60 * 1024 * 1024),
        cost_estimate=pl.CostEstimate(flops=flops, bytes_accessed=12 << 20, transcendentals=0),
    )(*args)


def conv_scratch(rows, cols, chans):
    tiles = (rows // TR) * (cols // TC)
    return [
        pltpu.VMEM((rows + TR, cols + 2 * OFF, chans), F32),
        pltpu.VMEM(((cols // 8 + 1) * chans * (rows // TR + 1), LANES), F32),
        pltpu.VMEM((chans * (tiles + 8), LANES), F32),
    ]


def masters(kernel_dw):
    flat = kernel_dw.reshape(KS * KS, -1)
    chans = flat.shape[1]
    hot = spread()
    out = []
    for each in (hot, hot[::-1]):
        wide = lax.dot_general(flat, jnp.asarray(each, BF16), TN, preferred_element_type=F32)
        out.append(wide.astype(BF16).reshape(chans * CHUNKS * 16, LANES))
    return out


def run_cells(tile, frame, cot, blocks, master, params):
    kernel_dw, bias_dw, gain, shift_ln, w_in, b_in, w_out = params
    rows, cols, chans = tile.shape
    hidden = w_in.shape[1]
    shape = jax.ShapeDtypeStruct

    def lanes(x):
        return jnp.broadcast_to(x[:, None], (x.shape[0], LANES))

    return call(
        cells_kernel,
        (
            shape(tile.shape, BF16),
            shape((chans, hidden), F32),
            shape((hidden, chans), F32),
            shape((chans, 3), F32),
            shape((hidden, 1), F32),
            shape((LANES, chans), F32),
        ),
        conv_scratch(rows, cols, chans)
        + [
            pltpu.VMEM((3, chans, LANES), F32),
            pltpu.VMEM((hidden, LANES), F32),
            pltpu.VMEM((2, chans * 8, LANES), F32),
        ],
        4 * KS * KS * rows * cols * chans * 128,
        blocks, tile, *frame, cot, master, jnp.asarray(row_masks(), BF16), lanes(bias_dw), lanes(gain),
        lanes(shift_ln), w_in.T, lanes(b_in), w_out, w_in, jnp.asarray(gather_taps(), F32),
        scalars=(0,),
    )


def run_input(dy, frame, cot, master, kernel_dw, is_north):
    rows, cols, chans = dy.shape
    taps = jnp.broadcast_to(kernel_dw.astype(F32).reshape(KS * KS, 1, chans), (KS * KS, 8, chans))
    return call(
        input_kernel,
        jax.ShapeDtypeStruct(dy.shape, BF16),
        conv_scratch(rows, cols, chans)
        + [
            pltpu.VMEM((HALF, cols + 2 * OFF, chans), F32),
            pltpu.VMEM((HALF, cols, chans), F32),
        ],
        2 * KS * KS * rows * cols * chans * 128,
        dy, *frame, cot, master, jnp.asarray(row_masks(), BF16), taps, is_north,
        scalars=(9,),
    )


def axis_sum(x, axis):
    count = lax.axis_size(axis)
    if count & (count - 1):
        return lax.psum(x, axis)
    step = 1
    while step < count:
        x = x + lax.ppermute(x, axis, [(i, i ^ step) for i in range(count)])
        step *= 2
    return x


def dp_share(x, share):
    count, at = lax.axis_size("dp"), lax.axis_index("dp")
    if count != 2:
        return lax.dynamic_slice_in_dim(lax.psum(x, "dp"), at * share, share, 0)
    mine = lax.dynamic_slice_in_dim(x, at * share, share, 0)
    theirs = lax.dynamic_slice_in_dim(x, (1 - at) * share, share, 0)
    return mine + lax.ppermute(theirs, "dp", [(0, 1), (1, 0)])


def local(inputs, cotangent, kernel_dw, bias_dw, gain, shift_ln, w_in, b_in, w_out, ocean_mask):
    batch, rows, cols, chans = inputs.shape
    hidden = w_in.shape[1]
    params = (kernel_dw, bias_dw, gain, shift_ln, w_in, b_in, w_out)
    master, flipped = masters(kernel_dw)
    blocks = ocean_mask.reshape(-1)
    northern = lax.axis_index("lat") == lax.axis_size("lat") - 1
    is_north = jnp.where(northern, 1.0, 0.0).astype(F32).reshape(1)
    in_share = chans // lax.axis_size("dp")
    out_share = hidden // lax.axis_size("dp")
    sums, grads = None, []
    for n in range(batch):
        tile, cot = inputs[n], cotangent[n]
        edge = row_halo(tile)
        frame = (*edge, *column_halo(tile, *edge))
        dy, g_in, g_out, g_chan, g_bin, g_taps = run_cells(tile, frame, cot, blocks, master, params)
        south, north = row_halo(dy)
        strips = column_halo(dy, south, north)
        grads.append(run_input(dy, (south, north, *strips), cot, flipped, kernel_dw, is_north))
        small = jnp.concatenate([g_chan.T, g_bin.reshape(-1, chans), g_taps[: KS * KS]], 0)
        own = jnp.concatenate(
            [dp_share(g_in, in_share).reshape(-1, chans), dp_share(g_out, out_share), axis_sum(small, "dp")], 0
        )
        sums = own if sums is None else sums + own
    total = axis_sum(axis_sum(sums, "lat"), "lon")
    cells_all = lax.axis_size("dp") * batch * lax.axis_size("lat") * rows * lax.axis_size("lon") * cols
    scale = 1.0 / math.sqrt(cells_all)
    in_rows = in_share * hidden // chans
    parts = jnp.split(total, (in_rows, in_rows + out_share, in_rows + out_share + 3, total.shape[0] - KS * KS))
    s_in, s_out, s_chan, s_bin, s_taps = parts
    s_in, s_bin = s_in.reshape(in_share, hidden), s_bin.reshape(1, hidden)
    return (
        jnp.stack(grads),
        s_in * scale,
        s_out * scale,
        s_taps.reshape(KS, KS, chans) * scale,
        s_chan[2] * scale,
        s_chan[0] * scale,
        s_chan[1] * scale,
        s_bin[0] * scale,
    )


def solution(mesh):
    field = P(("groups", "dp"), "lat", "lon", None)
    placed = (field, field, P(), P(), P(), P(), P(), P(), P(), P("lat", "lon"))
    return jax.shard_map(
        local,
        mesh=mesh,
        in_specs=placed,
        out_specs=(
            field,
            P(("groups", "dp"), None),
            P(("groups", "dp"), None),
            P("groups", None, None),
            P("groups"),
            P("groups"),
            P("groups"),
            P("groups"),
        ),
        check_vma=False,
    )
```

```python
import math

import jax
import jax.numpy as jnp
import numpy as np
from jax import lax
from jax.experimental import pallas as pl
from jax.experimental.pallas import tpu as pltpu
from jax.sharding import PartitionSpec as P

KS = 7
HALF = 3
EPS = 1e-06
GELU_K = 0.7978845608
GELU_C = 0.044715
F32 = jnp.float32
BF16 = jnp.bfloat16
TR = 8
TC = 16
LANES = TR * TC
CHUNKS = TC // 8 + 1
DEPTH = CHUNKS * LANES
OFF = 8
SIDE = 4
MESH = pl.DeviceIdType.MESH
STRIP = 16
NT = (((1,), (1,)), ((), ()))
TN = (((0,), (0,)), ((), ()))


def spread():
    jb, ri, ji, ro, jo = np.meshgrid(*(np.arange(n) for n in (CHUNKS, 2, 8, TR, TC)), indexing="ij")
    a = (ri - ro) % 8
    b = 8 * jb + ji - jo - 1
    tap = np.where((a < KS) & (b >= 0) & (b < KS), a * KS + b, -1)
    hot = tap.reshape(1, -1) == np.arange(KS * KS)[:, None]
    return hot.astype(np.float32)


def row_masks():
    p, ri, ji, ro, jo = np.meshgrid(*(np.arange(n) for n in (4, 2, 8, TR, TC)), indexing="ij")
    low = (ro <= 2 * p + ri).reshape(4, 1, 16, LANES)
    both = np.concatenate([low, ~low], 0).astype(np.float32)
    return np.broadcast_to(both, (8, CHUNKS, 16, LANES)).reshape(8 * CHUNKS * 16, LANES)


def gather_taps():
    s, jb, ri, ji = np.meshgrid(*(np.arange(n) for n in (8, 2, 16, 8)), indexing="ij")
    b = 8 * jb + ji - s - 1
    tap = np.where((ri < KS) & (b >= 0) & (b < KS), ri * KS + b, -1)
    return (tap.reshape(-1, 1) == np.arange(LANES)[None]).astype(np.float32)


def load_extended(ext, tile, south, north, west, east):
    rows, cols, chans = tile.shape

    def fill(r, carry):
        ext[r + HALF, OFF : OFF + cols, :] = tile[r].astype(F32)
        return carry

    lax.fori_loop(0, rows, fill, 0, unroll=2)
    for m in range(HALF):
        ext[m, OFF : OFF + cols, :] = south[m].astype(F32)
        ext[rows + HALF + m, OFF : OFF + cols, :] = north[m].astype(F32)
    for m in range(rows + 2 * HALF, ext.shape[0]):
        ext[m] = jnp.zeros(ext.shape[1:], F32)

    def sides(k, carry):
        left, right = west[k].astype(F32), east[k].astype(F32)
        for n in range(4):
            ext[4 * k + n, OFF - SIDE : OFF, :] = left[SIDE * n : SIDE * n + SIDE]
            ext[4 * k + n, OFF + cols : OFF + cols + SIDE, :] = right[SIDE * n : SIDE * n + SIDE]
        return carry

    lax.fori_loop(0, west.shape[0], sides, 0)


def make_patches(ext, patches, rows, cols):
    bands = rows // TR
    chans = ext.shape[-1]
    step = bands + 1

    def piece(jc):
        at = pl.multiple_of(jc * 8, 8) + (OFF - 4)
        for q in range(bands):
            block = jnp.concatenate([ext[q * TR + k, pl.ds(at, 8), :] for k in range(2 * TR)], 0)
            turned = block.astype(BF16).T.astype(F32)
            patches[pl.ds(jc * (chans * step) + q, chans, stride=step), :] = turned

    def pieces(jc, carry):
        piece(jc)
        return carry

    lax.fori_loop(0, cols // 8, pieces, 0, unroll=4)
    piece(cols // 8)


def patch_rows(patches, c, chans, bands, across):
    step = bands + 1

    def block(jc):
        return patches[pl.ds(jc * (chans * step) + c * step, bands), :]

    parts = []
    for jb in range(CHUNKS):
        parts.append(jnp.concatenate([block(2 * u + jb) for u in range(across)], 0).astype(BF16))
    return jnp.concatenate(parts, 1)


def conv_patches(patches, master, masks, y, chans, bands, across, pitch):
    width = CHUNKS * 16

    def channel(c, carry):
        base = master[pl.ds(pl.multiple_of(c * width, width), width), :]
        turned = [base] + [pltpu.roll(base, 32 * s, 1) for s in range(1, 4)]
        strips = [turned[p % 4] * masks[p * width : (p + 1) * width, :] for p in range(8)]
        weights = jnp.concatenate(
            [strips[p][16 * jb : 16 * jb + 16] for jb in range(CHUNKS) for p in range(8)], 0
        )
        rows = patch_rows(patches, c, chans, bands, across)
        y[pl.ds(pl.multiple_of(c * pitch, 8), bands * across), :] = jnp.dot(
            rows, weights, preferred_element_type=F32
        )
        return carry

    lax.fori_loop(0, chans, channel, 0, unroll=16)


def cells_kernel(
    blocks, tile, south, north, west, east, cot, master, masks, bias, gain, shift, w_in_t, b_in, w_out, w_in,
    gather,
    dy, g_in, g_out, g_chan, g_bin, g_taps,
    ext, patches, y, s_chan, s_bin, s_taps,
):
    rows, cols, chans = tile.shape
    hidden = w_out.shape[0]
    bands, across = rows // TR, cols // TC
    tiles = bands * across
    pitch = tiles + 8
    per_block = across // blocks.shape[0]
    load_extended(ext, tile, south, north, west, east)
    make_patches(ext, patches, rows, cols)
    conv_patches(patches, master, masks, y, chans, bands, across, pitch)
    g_in[...] = jnp.zeros_like(g_in)
    g_out[...] = jnp.zeros_like(g_out)
    s_chan[...] = jnp.zeros_like(s_chan)
    s_bin[...] = jnp.zeros_like(s_bin)
    inv = 1.0 / chans

    wide = bands * LANES
    bias_rows, gain_rows, shift_rows = bias[...], gain[...], shift[...]

    def fold_lanes(x):
        total = x[:, :LANES]
        for k in range(1, bands):
            total = total + x[:, k * LANES : (k + 1) * LANES]
        return total

    def step(u, carry):
        t = u * bands
        nhats, rstds, parts = [], [], []
        for k in range(bands):
            yc = y[pl.ds(t + k, chans, stride=pitch), :] + bias_rows
            center = yc - jnp.sum(yc, 0, keepdims=True) * inv
            rstd = lax.rsqrt(jnp.sum(center * center, 0, keepdims=True) * inv + EPS)
            nhat = center * rstd
            nhats.append(nhat)
            rstds.append(rstd)
            parts.append((nhat * gain_rows + shift_rows).astype(BF16))
        normed = jnp.concatenate(parts, 1)
        at = pl.ds(pl.multiple_of(u * TC, TC), TC)
        sea = blocks[u // per_block].astype(F32).astype(BF16)
        og = cot[:, at, :].reshape(wide, chans) * sea
        pre_all = jnp.dot(w_in_t[...], normed, preferred_element_type=F32)
        dact_all = lax.dot_general(w_out[...], og, NT, preferred_element_type=F32)
        acts, dpres = [], []
        for r in range(0, hidden, STRIP):
            own = slice(r, r + STRIP)
            pre = pre_all[own] + jnp.concatenate([b_in[own, :]] * bands, 1)
            square = pre * pre
            th = jnp.tanh(pre * (GELU_K + (GELU_K * GELU_C) * square))
            h = 0.5 + 0.5 * th
            act = pre * h
            slope = h + act * (1.0 - h) * (2.0 * GELU_K + (6.0 * GELU_K * GELU_C) * square)
            dpre = dact_all[own] * slope
            s_bin[own, :] += fold_lanes(dpre)
            acts.append(act.astype(BF16))
            dpres.append(dpre.astype(BF16))
        act_b, dpre_b = jnp.concatenate(acts, 0), jnp.concatenate(dpres, 0)
        g_out[...] += jnp.dot(act_b, og, preferred_element_type=F32)
        g_in[...] += lax.dot_general(normed, dpre_b, NT, preferred_element_type=F32)
        dnorm_all = jnp.dot(w_in[...], dpre_b, preferred_element_type=F32)
        sums = [None] * 3
        for k in range(bands):
            dnorm = dnorm_all[:, k * LANES : (k + 1) * LANES]
            nhat = nhats[k]
            scaled = dnorm * nhat
            dn = dnorm * gain_rows
            m1 = jnp.sum(dn, 0, keepdims=True) * inv
            m2 = jnp.sum(dn * nhat, 0, keepdims=True) * inv
            delta_b = (rstds[k] * (dn - m1 - nhat * m2)).astype(BF16)
            delta = delta_b.astype(F32)
            sums = [new if old is None else old + new for old, new in zip(sums, (scaled, dnorm, delta))]
            y[pl.ds(t + k, chans, stride=pitch), :] = delta
            dy[k * TR : (k + 1) * TR, at, :] = delta_b.T.reshape(TR, TC, chans)
        for n in range(3):
            s_chan[n] += sums[n]
        return carry

    lax.fori_loop(0, across, step, 0)
    for n in range(3):
        g_chan[:, n : n + 1] = jnp.sum(s_chan[n], axis=1, keepdims=True)
    g_bin[...] = jnp.sum(s_bin[...], axis=1, keepdims=True)

    def channel(c, carry):
        delta = y[pl.ds(pl.multiple_of(c * pitch, 8), tiles), :].astype(BF16)
        found = lax.dot_general(
            delta, patch_rows(patches, c, chans, bands, across), TN, preferred_element_type=F32
        )
        for jb in range(2):
            acc = None
            for ro in range(TR):
                term = None
                for h in range(TC // 8):
                    at = ro * TC + 8 * h
                    piece = found[at : at + 8, (jb + h) * LANES : (jb + h + 1) * LANES]
                    term = piece if term is None else term + piece
                term = pltpu.roll(term, (LANES - 8 * ro) % LANES, 1) if ro else term
                acc = term if acc is None else acc + term
            s_taps[jb, pl.ds(pl.multiple_of(c * 8, 8), 8), :] = acc
        return carry

    lax.fori_loop(0, chans, channel, 0, unroll=16)
    total = None
    for s in range(8):
        for jb in range(2):
            term = jnp.dot(
                s_taps[jb, pl.ds(s, chans, stride=8), :],
                gather[(2 * s + jb) * LANES : (2 * s + jb + 1) * LANES, :],
                precision=lax.Precision.HIGHEST,
                preferred_element_type=F32,
            )
            total = term if total is None else total + term
    g_taps[...] = total.T


def input_kernel(
    tile, south, north, west, east, cot, master, masks, taps, is_north,
    out,
    ext, patches, y, fold, folded,
):
    rows, cols, chans = tile.shape
    bands, across = rows // TR, cols // TC
    tiles = bands * across
    pitch = tiles + 8
    load_extended(ext, tile, south, north, west, east)
    flag = is_north[0]
    for m in range(HALF):
        row = ext[rows + HALF + m]
        fold[m] = row * flag
        ext[rows + HALF + m] = row * (1.0 - flag)

    def fold_step(i, carry):
        c0 = pl.multiple_of(i * TC, TC)
        for m in range(HALF):
            acc = jnp.zeros((TC // 8, 8, chans), F32)
            for n in range(m + 1):
                a = KS - 1 - m + n
                for b in range(KS):
                    v = fold[n, pl.ds(c0 + (OFF - HALF + b), TC), :]
                    acc = acc + v.reshape(TC // 8, 8, chans) * taps[a * KS + b][None]
            folded[m, pl.ds(c0, TC), :] = acc.reshape(TC, chans)
        return carry

    lax.fori_loop(0, cols // TC, fold_step, 0)
    make_patches(ext, patches, rows, cols)
    conv_patches(patches, master, masks, y, chans, bands, across, pitch)

    def step(u, carry):
        at = pl.ds(pl.multiple_of(u * TC, TC), TC)
        for q in range(bands):
            direct = y[pl.ds(u * bands + q, chans, stride=pitch), :].T.reshape(TR, TC, chans)
            total = direct + cot[q * TR : (q + 1) * TR, at, :].astype(F32)
            if q == bands - 1:
                out[q * TR : rows - HALF, at, :] = total[: TR - HALF].astype(BF16)
                out[rows - HALF : rows, at, :] = (total[TR - HALF :] + folded[:, at, :]).astype(BF16)
            else:
                out[q * TR : (q + 1) * TR, at, :] = total.astype(BF16)
        return carry

    lax.fori_loop(0, across, step, 0)


def frame_kernel(
    tile, south, north, west, east,
    edges, sides, rows_in, cols_in, packed, strip, local_sem, send_sem, recv_sem,
):
    rows, cols, chans = tile.shape
    lat, lats = lax.axis_index("lat"), lax.axis_size("lat")
    lon, lons = lax.axis_index("lon"), lax.axis_size("lon")
    top = lats - 1
    above = {"lat": jnp.minimum(lat + 1, top)}
    below = {"lat": jnp.maximum(lat - 1, 0)}
    mirror = {"lon": lons - 1 - lon}
    west_of, east_of = {"lon": lax.rem(lon + lons - 1, lons)}, {"lon": lax.rem(lon + 1, lons)}
    own = [
        pltpu.make_async_copy(tile.at[pl.ds(0, HALF)], edges.at[0], local_sem.at[0]),
        pltpu.make_async_copy(tile.at[pl.ds(rows - HALF, HALF)], edges.at[1], local_sem.at[1]),
        pltpu.make_async_copy(tile.at[:, pl.ds(0, 16)], sides.at[0], local_sem.at[2]),
        pltpu.make_async_copy(tile.at[:, pl.ds(cols - 16, 16)], sides.at[1], local_sem.at[3]),
    ]
    for copy in own:
        copy.start()
    barrier = pltpu.get_barrier_semaphore()
    for device in (west_of, east_of):
        pl.semaphore_signal(barrier, inc=1, device_id=device, device_id_type=MESH)

    @pl.when(lat > 0)
    def _():
        pl.semaphore_signal(barrier, inc=1, device_id=below, device_id_type=MESH)

    @pl.when(lat < top)
    def _():
        pl.semaphore_signal(barrier, inc=1, device_id=above, device_id_type=MESH)

    @pl.when(lat == top)
    def _():
        pl.semaphore_signal(barrier, inc=1, device_id=mirror, device_id_type=MESH)

    pl.semaphore_wait(barrier, 3 + jnp.minimum(lat, 1))

    def send(source, target, n, device):
        return pltpu.make_async_remote_copy(
            src_ref=source, dst_ref=target, send_sem=send_sem.at[n], recv_sem=recv_sem.at[n],
            device_id=device, device_id_type=MESH,
        )

    up = send(edges.at[1], rows_in.at[0], 0, above)
    down = send(edges.at[0], rows_in.at[1], 1, below)
    over = send(edges.at[1], rows_in.at[1], 2, mirror)
    own[0].wait()
    own[1].wait()

    @pl.when(lat < top)
    def _():
        up.start()

    @pl.when(lat > 0)
    def _():
        down.start()

    @pl.when(lat == top)
    def _():
        over.start()

    own[2].wait()
    own[3].wait()

    def fill(r, carry):
        at = pl.ds(pl.multiple_of((r + HALF + 1) * 8, 8), 8)
        strip[0, at, :] = sides[0, r].astype(F32)[:8]
        strip[1, at, :] = sides[1, r].astype(F32)[8:]
        return carry

    lax.fori_loop(0, rows, fill, 0, unroll=4)
    blank = jnp.zeros((8, chans), F32)
    for e in (-1, rows + 2 * HALF, rows + 2 * HALF + 1, rows + 2 * HALF + 2):
        for side in range(2):
            strip[side, (e + 1) * 8 : (e + 2) * 8, :] = blank

    @pl.when(lat > 0)
    def _():
        up.wait_recv()
        south[...] = rows_in[0]

    @pl.when(lat == 0)
    def _():
        south[...] = jnp.zeros(south.shape, BF16)

    @pl.when(lat < top)
    def _():
        down.wait_recv()
        north[...] = rows_in[1]

    @pl.when(lat == top)
    def _():
        over.wait_recv()
        shape = (cols, cols)
        swap = lax.broadcasted_iota(jnp.int32, shape, 0) + lax.broadcasted_iota(jnp.int32, shape, 1) == cols - 1
        swap = jnp.where(swap, 1.0, 0.0).astype(BF16)
        for m in range(HALF):
            turned = jnp.dot(swap, rows_in[1, HALF - 1 - m], preferred_element_type=F32)
            north[m] = turned.astype(BF16)

    for first, halo in ((0, south), (rows + HALF, north)):
        for m in range(HALF):
            at = slice((first + m + 1) * 8, (first + m + 2) * 8)
            strip[0, at, :] = halo[m, :16, :].astype(F32)[:8]
            strip[1, at, :] = halo[m, cols - 16 :, :].astype(F32)[8:]
    low = lax.broadcasted_iota(jnp.int32, (8, chans), 0) < SIDE

    def pack(k, carry):
        for side in range(2):
            halves = []
            for n in range(0, 4, 2):
                at = pl.multiple_of((4 * k + n + 1) * 8, 8) + SIDE * side
                even = strip[side, pl.ds(at, 8), :]
                odd = strip[side, pl.ds(at + 8 - SIDE, 8), :]
                halves.append(jnp.where(low, even, odd))
            packed[side, k] = jnp.concatenate(halves, 0).astype(BF16)
        return carry

    lax.fori_loop(0, packed.shape[1], pack, 0, unroll=3)
    to_west = send(packed.at[0], cols_in.at[1], 3, west_of)
    to_east = send(packed.at[1], cols_in.at[0], 4, east_of)
    to_west.start()
    to_east.start()
    to_east.wait_recv()
    west[...] = cols_in[0]
    to_west.wait_recv()
    east[...] = cols_in[1]
    to_west.wait_send()
    to_east.wait_send()

    @pl.when(lat < top)
    def _():
        up.wait_send()

    @pl.when(lat > 0)
    def _():
        down.wait_send()

    @pl.when(lat == top)
    def _():
        over.wait_send()


def frame_of(tile, collective_id):
    rows, cols, chans = tile.shape
    vmem = pl.BlockSpec(memory_space=pltpu.VMEM)
    groups = (rows + TR) // 4
    shape = jax.ShapeDtypeStruct
    return pl.pallas_call(
        frame_kernel,
        out_shape=(shape((HALF, cols, chans), BF16),) * 2 + (shape((groups, 16, chans), BF16),) * 2,
        in_specs=[pl.BlockSpec(memory_space=pl.ANY)],
        out_specs=(vmem,) * 4,
        scratch_shapes=[
            pltpu.VMEM((2, HALF, cols, chans), BF16),
            pltpu.VMEM((2, rows, 16, chans), BF16),
            pltpu.VMEM((2, HALF, cols, chans), BF16),
            pltpu.VMEM((2, groups, 16, chans), BF16),
            pltpu.VMEM((2, groups, 16, chans), BF16),
            pltpu.VMEM((2, (rows + TR + 2) * 8, chans), F32),
            pltpu.SemaphoreType.DMA((4,)),
            pltpu.SemaphoreType.DMA((5,)),
            pltpu.SemaphoreType.DMA((5,)),
        ],
        compiler_params=pltpu.CompilerParams(
            collective_id=collective_id, has_side_effects=True, vmem_limit_bytes=16 * 1024 * 1024
        ),
        cost_estimate=pl.CostEstimate(flops=1 << 20, bytes_accessed=4 << 20, transcendentals=0),
    )(tile)


def call(kernel, out_shape, scratch, flops, *args, scalars=()):
    vmem = pl.BlockSpec(memory_space=pltpu.VMEM)
    smem = pl.BlockSpec(memory_space=pltpu.SMEM)
    return pl.pallas_call(
        kernel,
        out_shape=out_shape,
        in_specs=[smem if n in scalars else vmem for n in range(len(args))],
        out_specs=jax.tree.map(lambda _: vmem, out_shape),
        scratch_shapes=scratch,
        compiler_params=pltpu.CompilerParams(vmem_limit_bytes=60 * 1024 * 1024),
        cost_estimate=pl.CostEstimate(flops=flops, bytes_accessed=12 << 20, transcendentals=0),
    )(*args)


def conv_scratch(rows, cols, chans):
    tiles = (rows // TR) * (cols // TC)
    return [
        pltpu.VMEM((rows + TR, cols + 2 * OFF, chans), F32),
        pltpu.VMEM(((cols // 8 + 1) * chans * (rows // TR + 1), LANES), F32),
        pltpu.VMEM((chans * (tiles + 8), LANES), F32),
    ]


def masters(kernel_dw):
    flat = kernel_dw.reshape(KS * KS, -1)
    chans = flat.shape[1]
    hot = spread()
    out = []
    for each in (hot, hot[::-1]):
        wide = lax.dot_general(flat, jnp.asarray(each, BF16), TN, preferred_element_type=F32)
        out.append(wide.astype(BF16).reshape(chans * CHUNKS * 16, LANES))
    return out


def run_cells(tile, frame, cot, blocks, master, params):
    kernel_dw, bias_dw, gain, shift_ln, w_in, b_in, w_out = params
    rows, cols, chans = tile.shape
    hidden = w_in.shape[1]
    shape = jax.ShapeDtypeStruct

    def lanes(x):
        return jnp.broadcast_to(x[:, None], (x.shape[0], LANES))

    return call(
        cells_kernel,
        (
            shape(tile.shape, BF16),
            shape((chans, hidden), F32),
            shape((hidden, chans), F32),
            shape((chans, 3), F32),
            shape((hidden, 1), F32),
            shape((LANES, chans), F32),
        ),
        conv_scratch(rows, cols, chans)
        + [
            pltpu.VMEM((3, chans, LANES), F32),
            pltpu.VMEM((hidden, LANES), F32),
            pltpu.VMEM((2, chans * 8, LANES), F32),
        ],
        4 * KS * KS * rows * cols * chans * 128,
        blocks, tile, *frame, cot, master, jnp.asarray(row_masks(), BF16), lanes(bias_dw), lanes(gain),
        lanes(shift_ln), w_in.T, lanes(b_in), w_out, w_in, jnp.asarray(gather_taps(), F32),
        scalars=(0,),
    )


def run_input(dy, frame, cot, master, kernel_dw, is_north):
    rows, cols, chans = dy.shape
    taps = jnp.broadcast_to(kernel_dw.astype(F32).reshape(KS * KS, 1, chans), (KS * KS, 8, chans))
    return call(
        input_kernel,
        jax.ShapeDtypeStruct(dy.shape, BF16),
        conv_scratch(rows, cols, chans)
        + [
            pltpu.VMEM((HALF, cols + 2 * OFF, chans), F32),
            pltpu.VMEM((HALF, cols, chans), F32),
        ],
        2 * KS * KS * rows * cols * chans * 128,
        dy, *frame, cot, master, jnp.asarray(row_masks(), BF16), taps, is_north,
        scalars=(9,),
    )


def axis_sum(x, axis):
    count = lax.axis_size(axis)
    if count & (count - 1):
        return lax.psum(x, axis)
    step = 1
    while step < count:
        x = x + lax.ppermute(x, axis, [(i, i ^ step) for i in range(count)])
        step *= 2
    return x


def dp_share(x, share):
    count, at = lax.axis_size("dp"), lax.axis_index("dp")
    if count != 2:
        return lax.dynamic_slice_in_dim(lax.psum(x, "dp"), at * share, share, 0)
    mine = lax.dynamic_slice_in_dim(x, at * share, share, 0)
    theirs = lax.dynamic_slice_in_dim(x, (1 - at) * share, share, 0)
    return mine + lax.ppermute(theirs, "dp", [(0, 1), (1, 0)])


def local(inputs, cotangent, kernel_dw, bias_dw, gain, shift_ln, w_in, b_in, w_out, ocean_mask):
    batch, rows, cols, chans = inputs.shape
    hidden = w_in.shape[1]
    params = (kernel_dw, bias_dw, gain, shift_ln, w_in, b_in, w_out)
    master, flipped = masters(kernel_dw)
    blocks = ocean_mask.reshape(-1)
    northern = lax.axis_index("lat") == lax.axis_size("lat") - 1
    is_north = jnp.where(northern, 1.0, 0.0).astype(F32).reshape(1)
    in_share = chans // lax.axis_size("dp")
    out_share = hidden // lax.axis_size("dp")
    sums, grads = None, []
    for n in range(batch):
        tile, cot = inputs[n], cotangent[n]
        frame = frame_of(tile, 0)
        dy, g_in, g_out, g_chan, g_bin, g_taps = run_cells(tile, frame, cot, blocks, master, params)
        grads.append(run_input(dy, frame_of(dy, 0), cot, flipped, kernel_dw, is_north))
        small = jnp.concatenate([g_chan.T, g_bin.reshape(-1, chans), g_taps[: KS * KS]], 0)
        own = jnp.concatenate(
            [dp_share(g_in, in_share).reshape(-1, chans), dp_share(g_out, out_share), axis_sum(small, "dp")], 0
        )
        sums = own if sums is None else sums + own
    total = axis_sum(axis_sum(sums, "lat"), "lon")
    cells_all = lax.axis_size("dp") * batch * lax.axis_size("lat") * rows * lax.axis_size("lon") * cols
    scale = 1.0 / math.sqrt(cells_all)
    in_rows = in_share * hidden // chans
    parts = jnp.split(total, (in_rows, in_rows + out_share, in_rows + out_share + 3, total.shape[0] - KS * KS))
    s_in, s_out, s_chan, s_bin, s_taps = parts
    s_in, s_bin = s_in.reshape(in_share, hidden), s_bin.reshape(1, hidden)
    return (
        jnp.stack(grads),
        s_in * scale,
        s_out * scale,
        s_taps.reshape(KS, KS, chans) * scale,
        s_chan[2] * scale,
        s_chan[0] * scale,
        s_chan[1] * scale,
        s_bin[0] * scale,
    )


def solution(mesh):
    field = P(("groups", "dp"), "lat", "lon", None)
    placed = (field, field, P(), P(), P(), P(), P(), P(), P(), P("lat", "lon"))
    return jax.shard_map(
        local,
        mesh=mesh,
        in_specs=placed,
        out_specs=(
            field,
            P(("groups", "dp"), None),
            P(("groups", "dp"), None),
            P("groups", None, None),
            P("groups"),
            P("groups"),
            P("groups"),
            P("groups"),
        ),
        check_vma=False,
    )
```

```python
import math

import jax
import jax.numpy as jnp
import numpy as np
from jax import lax
from jax.experimental import pallas as pl
from jax.experimental.pallas import tpu as pltpu
from jax.sharding import PartitionSpec as P

KS = 7
HALF = 3
EPS = 1e-06
GELU_K = 0.7978845608
GELU_C = 0.044715
F32 = jnp.float32
BF16 = jnp.bfloat16
TR = 8
TC = 16
LANES = TR * TC
CHUNKS = TC // 8 + 1
DEPTH = CHUNKS * LANES
OFF = 8
SIDE = 4
MESH = pl.DeviceIdType.MESH
STRIP = 16
NT = (((1,), (1,)), ((), ()))
TN = (((0,), (0,)), ((), ()))


def spread():
    jb, ri, ji, ro, jo = np.meshgrid(*(np.arange(n) for n in (CHUNKS, 2, 8, TR, TC)), indexing="ij")
    a = (ri - ro) % 8
    b = 8 * jb + ji - jo - 1
    tap = np.where((a < KS) & (b >= 0) & (b < KS), a * KS + b, -1)
    hot = tap.reshape(1, -1) == np.arange(KS * KS)[:, None]
    return hot.astype(np.float32)


def row_masks():
    p, ri, ji, ro, jo = np.meshgrid(*(np.arange(n) for n in (4, 2, 8, TR, TC)), indexing="ij")
    low = (ro <= 2 * p + ri).reshape(4, 1, 16, LANES)
    both = np.concatenate([low, ~low], 0).astype(np.float32)
    return np.broadcast_to(both, (8, CHUNKS, 16, LANES)).reshape(8 * CHUNKS * 16, LANES)


def gather_taps():
    s, jb, ri, ji = np.meshgrid(*(np.arange(n) for n in (8, 2, 16, 8)), indexing="ij")
    b = 8 * jb + ji - s - 1
    tap = np.where((ri < KS) & (b >= 0) & (b < KS), ri * KS + b, -1)
    return (tap.reshape(-1, 1) == np.arange(LANES)[None]).astype(np.float32)


def frame_ids():
    lat, lats = lax.axis_index("lat"), lax.axis_size("lat")
    lon, lons = lax.axis_index("lon"), lax.axis_size("lon")
    return (
        {"lon": lax.rem(lon + lons - 1, lons)},
        {"lon": lax.rem(lon + 1, lons)},
        {"lat": jnp.minimum(lat + 1, lats - 1)},
        {"lat": jnp.maximum(lat - 1, 0)},
        {"lon": lons - 1 - lon},
    )


def sum_route():
    route = []
    for axis in ("dp", "lat", "lon"):
        step = 1
        while step < lax.axis_size(axis):
            route.append((axis, step))
            step *= 2
    return route


def partner(axis, step):
    at = lax.axis_index(axis)
    return {axis: at + step * (1 - 2 * ((at // step) % 2))}


def block_kernel(
    blocks, tile, cot_far, master, masks, taps, bias, gain, shift, w_in, b_in, w_out, gather,
    out, o_in, o_out, o_taps, o_bias, o_gain, o_shift, o_bin,
    ext, patches, y, cot, normed_s, s_chan, s_bin, s_taps, g_in, g_out, columns, w_in_t,
    edges, rows_in, cols_in, packed, fold, folded, big, big_in, few, few_in,
    tile_sem, cot_sem, send_sem, recv_sem, big_send, big_recv, few_send, few_recv,
):
    rows, cols, chans = tile.shape
    hidden = w_out.shape[0]
    bands, across = rows // TR, cols // TC
    tiles = bands * across
    pitch = tiles + 8
    pieces = cols // 8 + 1
    step_rows = bands + 1
    wide = bands * LANES
    per_block = across // blocks.shape[1]
    lat, lats = lax.axis_index("lat"), lax.axis_size("lat")
    top = lats - 1
    west_of, east_of, above, below, mirror = frame_ids()
    route = sum_route()
    inv = 1.0 / chans

    depth = rows // 8
    loads = [
        pltpu.make_async_copy(tile.at[pl.ds(n * depth, depth)], out.at[pl.ds(n * depth, depth)], tile_sem.at[n])
        for n in range(8)
    ]
    for copy in loads:
        copy.start()
    cot_load = pltpu.make_async_copy(cot_far, cot, cot_sem)

    barrier = pltpu.get_barrier_semaphore()
    for device in (west_of, east_of):
        pl.semaphore_signal(barrier, inc=1, device_id=device, device_id_type=MESH)
    for axis, step in route:
        pl.semaphore_signal(barrier, inc=1, device_id=partner(axis, step), device_id_type=MESH)

    @pl.when(lat > 0)
    def _():
        pl.semaphore_signal(barrier, inc=1, device_id=below, device_id_type=MESH)

    @pl.when(lat < top)
    def _():
        pl.semaphore_signal(barrier, inc=1, device_id=above, device_id_type=MESH)

    @pl.when(lat == top)
    def _():
        pl.semaphore_signal(barrier, inc=1, device_id=mirror, device_id_type=MESH)

    pl.semaphore_wait(barrier, 3 + len(route) + jnp.minimum(lat, 1))

    def remote(source, target, sent, received, device):
        return pltpu.make_async_remote_copy(
            src_ref=source, dst_ref=target, send_sem=sent, recv_sem=received, device_id=device, device_id_type=MESH
        )

    def row_copies(n):
        if n:
            low, high = edges.at[0], edges.at[1]
        else:
            low, high = tile.at[pl.ds(0, HALF)], tile.at[pl.ds(rows - HALF, HALF)]
        sent, got = send_sem.at[n], recv_sem.at[n]
        return (
            (lat < top, remote(high, rows_in.at[n, 0], sent.at[0], got.at[0], above)),
            (lat > 0, remote(low, rows_in.at[n, 1], sent.at[1], got.at[1], below)),
            (lat == top, remote(high, rows_in.at[n, 1], sent.at[2], got.at[2], mirror)),
        )

    def start_rows(n):
        for wanted, copy in row_copies(n):
            pl.when(wanted)(copy.start)

    def finish_rows(n):
        (_, up), (_, down), (_, over) = row_copies(n)
        inside = slice(OFF, OFF + cols)

        @pl.when(lat > 0)
        def _():
            up.wait_recv()
            for m in range(HALF):
                ext[m, inside, :] = rows_in[n, 0, m].astype(F32)

        @pl.when(lat == 0)
        def _():
            for m in range(HALF):
                ext[m, inside, :] = jnp.zeros((cols, chans), F32)

        @pl.when(lat < top)
        def _():
            down.wait_recv()
            for m in range(HALF):
                ext[rows + HALF + m, inside, :] = rows_in[n, 1, m].astype(F32)

        @pl.when(lat == top)
        def _():
            over.wait_recv()
            shape = (cols, cols)
            swap = lax.broadcasted_iota(jnp.int32, shape, 0) + lax.broadcasted_iota(jnp.int32, shape, 1) == cols - 1
            swap = jnp.where(swap, 1.0, 0.0).astype(BF16)
            for m in range(HALF):
                ext[rows + HALF + m, inside, :] = jnp.dot(
                    swap, rows_in[n, 1, HALF - 1 - m], preferred_element_type=F32
                )

    def col_copies(n):
        sent, got = send_sem.at[n], recv_sem.at[n]
        return (
            remote(packed.at[n, 0], cols_in.at[n, 1], sent.at[3], got.at[3], west_of),
            remote(packed.at[n, 1], cols_in.at[n, 0], sent.at[4], got.at[4], east_of),
        )

    def start_cols(n):
        keep = lax.broadcasted_iota(jnp.int32, (8, chans), 0) < SIDE

        def pack(k, carry):
            for side, at in ((0, OFF), (1, OFF + cols - SIDE)):
                halves = []
                for m in range(0, 4, 2):
                    even = ext[4 * k + m, at : at + 8, :]
                    odd = ext[4 * k + m + 1, at - SIDE : at - SIDE + 8, :]
                    halves.append(jnp.where(keep, even, odd))
                packed[n, side, k] = jnp.concatenate(halves, 0).astype(BF16)
            return carry

        lax.fori_loop(0, packed.shape[2], pack, 0)
        for copy in col_copies(n):
            copy.start()

    def finish_cols(n):
        to_west, to_east = col_copies(n)
        to_west.wait_recv()
        to_east.wait_recv()

        def sides(k, carry):
            left, right = cols_in[n, 0, k].astype(F32), cols_in[n, 1, k].astype(F32)
            for m in range(4):
                ext[4 * k + m, OFF - SIDE : OFF, :] = left[SIDE * m : SIDE * m + SIDE]
                ext[4 * k + m, OFF + cols : OFF + cols + SIDE, :] = right[SIDE * m : SIDE * m + SIDE]
            return carry

        lax.fori_loop(0, packed.shape[2], sides, 0)
        to_west.wait_send()
        to_east.wait_send()
        for wanted, copy in row_copies(n):
            pl.when(wanted)(copy.wait_send)

    def sum_copy(few_or_big, k):
        buf, land, sent, got = few_or_big
        return remote(buf.at[k], land.at[k], sent.at[k], got.at[k], partner(*route[k]))

    def advance(which, k, mine=None):
        if k >= len(route):
            return
        buf, land = which[:2]
        copy = sum_copy(which, k)
        copy.wait_recv()
        if mine is None:
            buf[k + 1] = buf[k] + land[k]
        else:
            mine(k + 1)
        copy.wait_send()
        if k + 1 < len(route):
            sum_copy(which, k + 1).start()

    big_sum, few_sum = (big, big_in, big_send, big_recv), (few, few_in, few_send, few_recv)

    def piece(jc, which):
        at = pl.multiple_of(jc * 8, 8) + (OFF - 4)
        for q in which:
            block = jnp.concatenate([ext[q * TR + k, pl.ds(at, 8), :] for k in range(2 * TR)], 0)
            turned = block.astype(BF16).T.astype(F32)
            patches[pl.ds(jc * (chans * step_rows) + q, chans, stride=step_rows), :] = turned

    def make_patches(which):
        def body(jc, carry):
            piece(jc, which)
            return carry

        lax.fori_loop(0, pieces - 1, body, 0, unroll=4)

    def patch_rows(c):
        def block(jc):
            return patches[pl.ds(jc * (chans * step_rows) + c * step_rows, bands), :]

        parts = []
        for jb in range(CHUNKS):
            parts.append(jnp.concatenate([block(2 * u + jb) for u in range(across)], 0).astype(BF16))
        return jnp.concatenate(parts, 1)

    def conv(which, first, last):
        width = CHUNKS * 16

        def channel(c, carry):
            base = master[c, which * width : (which + 1) * width, :]
            turned = [base] + [pltpu.roll(base, 32 * s, 1) for s in range(1, 4)]
            strips = [turned[p % 4] * masks[p * width : (p + 1) * width, :] for p in range(8)]
            weights = jnp.concatenate(
                [strips[p][16 * jb : 16 * jb + 16] for jb in range(CHUNKS) for p in range(8)], 0
            )
            y[pl.ds(pl.multiple_of(c * pitch, 8), tiles), :] = jnp.dot(
                patch_rows(c), weights, preferred_element_type=F32
            )
            return carry

        lax.fori_loop(first, last, channel, 0, unroll=16)

    start_rows(0)
    cot_load.start()

    def column(n, x):
        columns[n] = jnp.broadcast_to(x, (LANES, chans)).T

    for n, x in enumerate((bias, gain, shift)):
        column(n, x[...])
    for n in range(hidden // chans):
        column(3 + n, b_in[:, n * chans : (n + 1) * chans])
    w_in_t[...] = w_in[...].T
    for m in range(rows + 2 * HALF, ext.shape[0]):
        ext[m] = jnp.zeros(ext.shape[1:], F32)
    for n in range(8):
        loads[n].wait()

        def fill(r, carry):
            ext[n * depth + r + HALF, OFF : OFF + cols, :] = out[n * depth + r].astype(F32)
            return carry

        lax.fori_loop(0, depth, fill, 0, unroll=2)
    make_patches(range(1, bands - 1))
    finish_rows(0)
    start_cols(0)
    make_patches((0, bands - 1))
    finish_cols(0)
    piece(0, range(bands))
    piece(pieces - 1, range(bands))
    conv(0, 0, chans)

    g_in[...] = jnp.zeros_like(g_in)
    g_out[...] = jnp.zeros_like(g_out)
    s_chan[...] = jnp.zeros_like(s_chan)
    s_bin[...] = jnp.zeros_like(s_bin)
    cot_load.wait()
    bias_rows, gain_rows, shift_rows = columns[0], columns[1], columns[2]

    def fold_lanes(x):
        total = x[:, :LANES]
        for k in range(1, bands):
            total = total + x[:, k * LANES : (k + 1) * LANES]
        return total

    def step(u, carry):
        t = u * bands
        nhats, rstds, parts = [], [], []
        for k in range(bands):
            yc = y[pl.ds(t + k, chans, stride=pitch), :] + bias_rows
            center = yc - jnp.sum(yc, 0, keepdims=True) * inv
            rstd = lax.rsqrt(jnp.sum(center * center, 0, keepdims=True) * inv + EPS)
            nhat = center * rstd
            nhats.append(nhat)
            rstds.append(rstd)
            parts.append((nhat * gain_rows + shift_rows).astype(BF16))
        normed = jnp.concatenate(parts, 1)
        start = pl.multiple_of(u * TC, TC)
        sea = blocks[0, u // per_block].astype(F32).astype(BF16)
        og = cot[:, pl.ds(start, TC), :].reshape(wide, chans) * sea
        pre_all = jnp.dot(w_in_t[...], normed, preferred_element_type=F32)
        dact_all = lax.dot_general(w_out[...], og, NT, preferred_element_type=F32)
        acts, dpres = [], []
        for r in range(0, hidden, STRIP):
            own = slice(r, r + STRIP)
            b_rows = columns[3 + r // chans, r % chans : r % chans + STRIP, :]
            pre = pre_all[own] + jnp.concatenate([b_rows] * bands, 1)
            square = pre * pre
            th = jnp.tanh(pre * (GELU_K + (GELU_K * GELU_C) * square))
            h = 0.5 + 0.5 * th
            act = pre * h
            slope = h + act * (1.0 - h) * (2.0 * GELU_K + (6.0 * GELU_K * GELU_C) * square)
            dpre = dact_all[own] * slope
            s_bin[own, :] += fold_lanes(dpre)
            acts.append(act.astype(BF16))
            dpres.append(dpre.astype(BF16))
        act_b, dpre_b = jnp.concatenate(acts, 0), jnp.concatenate(dpres, 0)
        g_out[...] += jnp.dot(act_b, og, preferred_element_type=F32)
        g_in[...] += lax.dot_general(normed, dpre_b, NT, preferred_element_type=F32)
        dnorm_all = jnp.dot(w_in[...], dpre_b, preferred_element_type=F32)
        sums = [None] * 3
        for k in range(bands):
            dnorm = dnorm_all[:, k * LANES : (k + 1) * LANES]
            nhat = nhats[k]
            scaled = dnorm * nhat
            dn = dnorm * gain_rows
            m1 = jnp.sum(dn, 0, keepdims=True) * inv
            m2 = jnp.sum(dn * nhat, 0, keepdims=True) * inv
            delta_b = (rstds[k] * (dn - m1 - nhat * m2)).astype(BF16)
            delta = delta_b.astype(F32)
            sums = [new if old is None else old + new for old, new in zip(sums, (scaled, dnorm, delta))]
            y[pl.ds(t + k, chans, stride=pitch), :] = delta
            ext[k * TR + HALF : (k + 1) * TR + HALF, pl.ds(start + OFF, TC), :] = (
                delta_b.T.astype(F32).reshape(TR, TC, chans)
            )
        for n in range(3):
            s_chan[n] += sums[n]
        return carry

    lax.fori_loop(0, across, step, 0)

    in_share, out_share = chans // 2, hidden // 2
    dp = lax.axis_index("dp")

    def shares(at, k, land=None):
        wanted = (
            (0, g_in, pl.ds(pl.multiple_of(at * in_share, 8), in_share), slice(0, chans)),
            (in_share, g_in, pl.ds(pl.multiple_of(at * in_share, 8), in_share), slice(chans, 2 * chans)),
            (2 * in_share, g_out, pl.ds(pl.multiple_of(at * out_share, 8), out_share), slice(0, chans)),
        )
        for first, ref, some, lanes in wanted:
            to = slice(first, first + some.size)
            value = ref[some, lanes]
            big[k, to, :] = value if land is None else value + big_in[land, to, :]

    small = 2 * in_share + out_share
    shares(1 - dp, 0)
    rest = [jnp.sum(s_chan[n].T, 0, keepdims=True) for n in range(3)]
    rest += [jnp.sum(s_bin[n * chans : (n + 1) * chans, :].T, 0, keepdims=True) for n in range(2)]
    rest = jnp.concatenate(rest + [jnp.zeros((3, chans), F32)], 0)
    big[0, small : small + 8, :] = rest
    sum_copy(big_sum, 0).start()
    for m in range(HALF):
        edges[0, m] = ext[HALF + m, OFF : OFF + cols, :].astype(BF16)
        edges[1, m] = ext[rows + m, OFF : OFF + cols, :].astype(BF16)
    start_rows(1)

    def first_sum(k):
        shares(dp, k, 0)
        to = slice(small, small + 8)
        big[k, to, :] = big[0, to, :] + big_in[0, to, :]

    def taps_of(first, last):
        def channel(c, carry):
            delta = y[pl.ds(pl.multiple_of(c * pitch, 8), tiles), :].astype(BF16)
            found = lax.dot_general(delta, patch_rows(c), TN, preferred_element_type=F32)
            for jb in range(2):
                acc = None
                for ro in range(TR):
                    term = None
                    for h in range(TC // 8):
                        at = ro * TC + 8 * h
                        some = found[at : at + 8, (jb + h) * LANES : (jb + h + 1) * LANES]
                        term = some if term is None else term + some
                    term = pltpu.roll(term, (LANES - 8 * ro) % LANES, 1) if ro else term
                    acc = term if acc is None else acc + term
                s_taps[jb, pl.ds(pl.multiple_of(c * 8, 8), 8), :] = acc
            return carry

        lax.fori_loop(first, last, channel, 0, unroll=16)

    quarter = chans // 4
    taps_of(0, quarter)
    finish_rows(1)
    start_cols(1)
    advance(big_sum, 0, first_sum)
    taps_of(quarter, 2 * quarter)
    finish_cols(1)
    advance(big_sum, 1)
    taps_of(2 * quarter, 3 * quarter)
    advance(big_sum, 2)
    taps_of(3 * quarter, chans)
    total = None
    for s in range(8):
        for jb in range(2):
            term = jnp.dot(
                s_taps[jb, pl.ds(s, chans, stride=8), :],
                gather[(2 * s + jb) * LANES : (2 * s + jb + 1) * LANES, :].astype(F32),
                precision=lax.Precision.HIGHEST,
                preferred_element_type=F32,
            )
            total = term if total is None else total + term
    few[0] = total.T[: few.shape[1]]
    sum_copy(few_sum, 0).start()
    advance(big_sum, 3)

    @pl.when(lat == top)
    def _():
        for m in range(HALF):
            fold[m] = ext[rows + HALF + m]
            ext[rows + HALF + m] = jnp.zeros(ext.shape[1:], F32)

        def fold_step(i, carry):
            c0 = pl.multiple_of(i * TC, TC)
            for m in range(HALF):
                acc = jnp.zeros((TC, chans), F32)
                for n in range(m + 1):
                    a = KS - 1 - m + n
                    for b in range(KS):
                        v = fold[n, pl.ds(c0 + (OFF - HALF + b), TC), :]
                        acc = acc + v * taps[a, b : b + 1, :].astype(F32)
                folded[m, pl.ds(c0, TC), :] = acc
            return carry

        lax.fori_loop(0, across, fold_step, 0)

    @pl.when(lat < top)
    def _():
        folded[...] = jnp.zeros_like(folded)

    make_patches(range(bands))
    piece(pieces - 1, range(bands))
    advance(few_sum, 0)
    conv(1, 0, chans // 2)
    advance(few_sum, 1)
    conv(1, chans // 2, chans)
    advance(few_sum, 2)

    def last_step(u, carry):
        at = pl.ds(pl.multiple_of(u * TC, TC), TC)
        for q in range(bands):
            direct = y[pl.ds(u * bands + q, chans, stride=pitch), :].T.reshape(TR, TC, chans)
            total = direct + cot[q * TR : (q + 1) * TR, at, :].astype(F32)
            if q == bands - 1:
                out[q * TR : rows - HALF, at, :] = total[: TR - HALF].astype(BF16)
                out[rows - HALF : rows, at, :] = (total[TR - HALF :] + folded[:, at, :]).astype(BF16)
            else:
                out[q * TR : (q + 1) * TR, at, :] = total.astype(BF16)
        return carry

    lax.fori_loop(0, across, last_step, 0)
    advance(few_sum, 3)
    for k in range(4, len(route)):
        advance(big_sum, k)
        advance(few_sum, k)
    end = len(route)
    cells_all = 2 * lats * rows * lax.axis_size("lon") * cols
    scale = 1.0 / math.sqrt(cells_all)
    o_in[:, :chans] = big[end, :in_share, :] * scale
    o_in[:, chans:] = big[end, in_share : 2 * in_share, :] * scale
    o_out[...] = big[end, 2 * in_share : small, :] * scale
    for n, ref in enumerate((o_gain, o_shift, o_bias)):
        ref[...] = big[end, small + n : small + n + 1, :] * scale
    o_bin[:, :chans] = big[end, small + 3 : small + 4, :] * scale
    o_bin[:, chans:] = big[end, small + 4 : small + 5, :] * scale
    for a in range(KS):
        o_taps[a] = few[end, a * KS : (a + 1) * KS, :] * scale


def local(inputs, cotangent, kernel_dw, bias_dw, gain, shift_ln, w_in, b_in, w_out, ocean_mask):
    _, rows, cols, chans = inputs.shape
    hidden = w_in.shape[1]
    hot = spread()
    both = np.concatenate([hot, hot[::-1]], 1).reshape(KS * KS, 2 * CHUNKS * 16, LANES)
    master = lax.dot_general(
        kernel_dw.reshape(KS * KS, chans), jnp.asarray(both, BF16), TN, preferred_element_type=F32
    ).astype(BF16)
    bands, across = rows // TR, cols // TC
    tiles = bands * across
    steps = len(sum_route())
    shape = jax.ShapeDtypeStruct
    vmem = pl.BlockSpec(memory_space=pltpu.VMEM)
    smem = pl.BlockSpec(memory_space=pltpu.SMEM)
    far = pl.BlockSpec(memory_space=pl.ANY)
    groups = (rows + TR) // 4
    big_rows, few_rows = chans + hidden // 2 + 8, 56
    dma = pltpu.SemaphoreType.DMA
    grad, s_in, s_out, s_taps, s_bias, s_gain, s_shift, s_bin = pl.pallas_call(
        block_kernel,
        out_shape=(
            shape((rows, cols, chans), BF16),
            shape((chans // 2, hidden), F32),
            shape((hidden // 2, chans), F32),
            shape((KS, KS, chans), F32),
            shape((1, chans), F32),
            shape((1, chans), F32),
            shape((1, chans), F32),
            shape((1, hidden), F32),
        ),
        in_specs=[smem, far, far] + [vmem] * 10,
        out_specs=(vmem,) * 8,
        scratch_shapes=[
            pltpu.VMEM((rows + TR, cols + 2 * OFF, chans), F32),
            pltpu.VMEM(((cols // 8 + 1) * chans * (bands + 1), LANES), F32),
            pltpu.VMEM((chans * (tiles + 8), LANES), F32),
            pltpu.VMEM((rows, cols, chans), BF16),
            pltpu.VMEM((8, LANES), F32),
            pltpu.VMEM((3, chans, LANES), F32),
            pltpu.VMEM((hidden, LANES), F32),
            pltpu.VMEM((2, chans * 8, LANES), F32),
            pltpu.VMEM((chans, hidden), F32),
            pltpu.VMEM((hidden, chans), F32),
            pltpu.VMEM((3 + hidden // chans, chans, LANES), F32),
            pltpu.VMEM((hidden, chans), BF16),
            pltpu.VMEM((2, HALF, cols, chans), BF16),
            pltpu.VMEM((2, 2, HALF, cols, chans), BF16),
            pltpu.VMEM((2, 2, groups, 16, chans), BF16),
            pltpu.VMEM((2, 2, groups, 16, chans), BF16),
            pltpu.VMEM((HALF, cols + 2 * OFF, chans), F32),
            pltpu.VMEM((HALF, cols, chans), F32),
            pltpu.VMEM((steps + 1, big_rows, chans), F32),
            pltpu.VMEM((steps, big_rows, chans), F32),
            pltpu.VMEM((steps + 1, few_rows, chans), F32),
            pltpu.VMEM((steps, few_rows, chans), F32),
            dma((8,)), dma, dma((2, 5)), dma((2, 5)),
            dma((steps,)), dma((steps,)), dma((steps,)), dma((steps,)),
        ],
        compiler_params=pltpu.CompilerParams(
            collective_id=0, has_side_effects=True, vmem_limit_bytes=63 * 1024 * 1024
        ),
        cost_estimate=pl.CostEstimate(flops=20 << 30, bytes_accessed=12 << 20, transcendentals=4 << 20),
    )(
        ocean_mask, inputs[0], cotangent[0], master, jnp.asarray(row_masks(), BF16), kernel_dw, bias_dw[None],
        gain[None], shift_ln[None], w_in, b_in[None], w_out, jnp.asarray(gather_taps(), BF16),
    )
    return grad[None], s_in, s_out, s_taps, s_bias[0], s_gain[0], s_shift[0], s_bin[0]


def solution(mesh):
    field = P(("groups", "dp"), "lat", "lon", None)
    placed = (field, field, P(), P(), P(), P(), P(), P(), P(), P("lat", "lon"))
    return jax.shard_map(
        local,
        mesh=mesh,
        in_specs=placed,
        out_specs=(
            field,
            P(("groups", "dp"), None),
            P(("groups", "dp"), None),
            P("groups", None, None),
            P("groups"),
            P("groups"),
            P("groups"),
            P("groups"),
        ),
        check_vma=False,
    )
```

```python
import functools
import math

import jax
import jax.numpy as jnp
import numpy as np
from jax import lax
from jax.experimental import pallas as pl
from jax.experimental.pallas import tpu as pltpu
from jax.sharding import PartitionSpec as P

KS = 7
HALF = 3
EPS = 1e-06
GELU_K = 0.7978845608
GELU_C = 0.044715
F32 = jnp.float32
BF16 = jnp.bfloat16
TR = 8
TC = 16
LANES = TR * TC
CHUNKS = TC // 8 + 1
DEPTH = CHUNKS * LANES
OFF = 8
SIDE = 4
MESH = pl.DeviceIdType.MESH
STRIP = 16
NT = (((1,), (1,)), ((), ()))
TN = (((0,), (0,)), ((), ()))


def spread():
    jb, ri, ji, ro, jo = np.meshgrid(*(np.arange(n) for n in (CHUNKS, 2, 8, TR, TC)), indexing="ij")
    a = (ri - ro) % 8
    b = 8 * jb + ji - jo - 1
    tap = np.where((a < KS) & (b >= 0) & (b < KS), a * KS + b, -1)
    hot = tap.reshape(1, -1) == np.arange(KS * KS)[:, None]
    return hot.astype(np.float32)


def row_masks():
    p, ri, ji, ro, jo = np.meshgrid(*(np.arange(n) for n in (4, 2, 8, TR, TC)), indexing="ij")
    low = (ro <= 2 * p + ri).reshape(4, 1, 16, LANES)
    both = np.concatenate([low, ~low], 0).astype(np.float32)
    return np.broadcast_to(both, (8, CHUNKS, 16, LANES)).reshape(8 * CHUNKS * 16, LANES)


def gather_taps():
    s, jb, ri, ji = np.meshgrid(*(np.arange(n) for n in (8, 2, 16, 8)), indexing="ij")
    b = 8 * jb + ji - s - 1
    tap = np.where((ri < KS) & (b >= 0) & (b < KS), ri * KS + b, -1)
    return (tap.reshape(-1, 1) == np.arange(LANES)[None]).astype(np.float32)


def frame_ids():
    lat, lats = lax.axis_index("lat"), lax.axis_size("lat")
    lon, lons = lax.axis_index("lon"), lax.axis_size("lon")
    return (
        {"lon": lax.rem(lon + lons - 1, lons)},
        {"lon": lax.rem(lon + 1, lons)},
        {"lat": jnp.minimum(lat + 1, lats - 1)},
        {"lat": jnp.maximum(lat - 1, 0)},
        {"lon": lons - 1 - lon},
    )


def sum_route():
    route = []
    for axis in ("dp", "lat", "lon"):
        step = 1
        while step < lax.axis_size(axis):
            route.append((axis, step))
            step *= 2
    return route


def partner(axis, step):
    at = lax.axis_index(axis)
    return {axis: at + step * (1 - 2 * ((at // step) % 2))}


def block_kernel(
    blocks, tile, cot_far, hot, masks, taps, bias, gain, shift, w_in, b_in, w_out, gather,
    out, totals,
    ext, patches, y, cot, master, s_chan, s_bin, s_taps, g_in, g_out, columns, w_in_t,
    edges, rows_in, cols_in, packed, fold, folded, big, big_in, few, few_in,
    tile_sem, cot_sem, send_sem, recv_sem, big_send, big_recv, few_send, few_recv,
):
    rows, cols, chans = tile.shape
    hidden = w_out.shape[0]
    bands, across = rows // TR, cols // TC
    tiles = bands * across
    pitch = tiles + 8
    pieces = cols // 8 + 1
    step_rows = bands + 1
    wide = bands * LANES
    per_block = across // blocks.shape[1]
    lat, lats = lax.axis_index("lat"), lax.axis_size("lat")
    top = lats - 1
    west_of, east_of, above, below, mirror = frame_ids()
    route = sum_route()
    inv = 1.0 / chans

    depth = rows // 8
    loads = [
        pltpu.make_async_copy(tile.at[pl.ds(n * depth, depth)], out.at[pl.ds(n * depth, depth)], tile_sem.at[n])
        for n in range(8)
    ]
    for copy in loads:
        copy.start()
    cot_load = pltpu.make_async_copy(cot_far, cot, cot_sem)

    barrier = pltpu.get_barrier_semaphore()
    for device in (west_of, east_of):
        pl.semaphore_signal(barrier, inc=1, device_id=device, device_id_type=MESH)
    for axis, step in route:
        pl.semaphore_signal(barrier, inc=1, device_id=partner(axis, step), device_id_type=MESH)

    @pl.when(lat > 0)
    def _():
        pl.semaphore_signal(barrier, inc=1, device_id=below, device_id_type=MESH)

    @pl.when(lat < top)
    def _():
        pl.semaphore_signal(barrier, inc=1, device_id=above, device_id_type=MESH)

    @pl.when(lat == top)
    def _():
        pl.semaphore_signal(barrier, inc=1, device_id=mirror, device_id_type=MESH)

    pl.semaphore_wait(barrier, 3 + len(route) + jnp.minimum(lat, 1))

    def remote(source, target, sent, received, device):
        return pltpu.make_async_remote_copy(
            src_ref=source, dst_ref=target, send_sem=sent, recv_sem=received, device_id=device, device_id_type=MESH
        )

    def row_copies(n):
        if n:
            low, high = edges.at[0], edges.at[1]
        else:
            low, high = tile.at[pl.ds(0, HALF)], tile.at[pl.ds(rows - HALF, HALF)]
        sent, got = send_sem.at[n], recv_sem.at[n]
        return (
            (lat < top, remote(high, rows_in.at[n, 0], sent.at[0], got.at[0], above)),
            (lat > 0, remote(low, rows_in.at[n, 1], sent.at[1], got.at[1], below)),
            (lat == top, remote(high, rows_in.at[n, 1], sent.at[2], got.at[2], mirror)),
        )

    def start_rows(n):
        for wanted, copy in row_copies(n):
            pl.when(wanted)(copy.start)

    def finish_rows(n):
        (_, up), (_, down), (_, over) = row_copies(n)
        inside = slice(OFF, OFF + cols)

        @pl.when(lat > 0)
        def _():
            up.wait_recv()
            for m in range(HALF):
                ext[m, inside, :] = rows_in[n, 0, m].astype(F32)

        @pl.when(lat == 0)
        def _():
            for m in range(HALF):
                ext[m, inside, :] = jnp.zeros((cols, chans), F32)

        @pl.when(lat < top)
        def _():
            down.wait_recv()
            for m in range(HALF):
                ext[rows + HALF + m, inside, :] = rows_in[n, 1, m].astype(F32)

        @pl.when(lat == top)
        def _():
            over.wait_recv()
            shape = (cols, cols)
            swap = lax.broadcasted_iota(jnp.int32, shape, 0) + lax.broadcasted_iota(jnp.int32, shape, 1) == cols - 1
            swap = jnp.where(swap, 1.0, 0.0).astype(BF16)
            for m in range(HALF):
                ext[rows + HALF + m, inside, :] = jnp.dot(
                    swap, rows_in[n, 1, HALF - 1 - m], preferred_element_type=F32
                )

    def col_copies(n):
        sent, got = send_sem.at[n], recv_sem.at[n]
        return (
            remote(packed.at[n, 0], cols_in.at[n, 1], sent.at[3], got.at[3], west_of),
            remote(packed.at[n, 1], cols_in.at[n, 0], sent.at[4], got.at[4], east_of),
        )

    def start_cols(n):
        keep = lax.broadcasted_iota(jnp.int32, (8, chans), 0) < SIDE

        def pack(k, carry):
            for side, at in ((0, OFF), (1, OFF + cols - SIDE)):
                halves = []
                for m in range(0, 4, 2):
                    even = ext[4 * k + m, at : at + 8, :]
                    odd = ext[4 * k + m + 1, at - SIDE : at - SIDE + 8, :]
                    halves.append(jnp.where(keep, even, odd))
                packed[n, side, k] = jnp.concatenate(halves, 0).astype(BF16)
            return carry

        lax.fori_loop(0, packed.shape[2], pack, 0)
        for copy in col_copies(n):
            copy.start()

    def finish_cols(n):
        to_west, to_east = col_copies(n)
        to_west.wait_recv()
        to_east.wait_recv()

        def sides(k, carry):
            left, right = cols_in[n, 0, k].astype(F32), cols_in[n, 1, k].astype(F32)
            for m in range(4):
                ext[4 * k + m, OFF - SIDE : OFF, :] = left[SIDE * m : SIDE * m + SIDE]
                ext[4 * k + m, OFF + cols : OFF + cols + SIDE, :] = right[SIDE * m : SIDE * m + SIDE]
            return carry

        lax.fori_loop(0, packed.shape[2], sides, 0)
        to_west.wait_send()
        to_east.wait_send()
        for wanted, copy in row_copies(n):
            pl.when(wanted)(copy.wait_send)

    def sum_copy(few_or_big, k):
        buf, land, sent, got = few_or_big
        return remote(buf.at[k], land.at[k], sent.at[k], got.at[k], partner(*route[k]))

    def advance(which, k, mine=None):
        if k >= len(route):
            return
        buf, land = which[:2]
        copy = sum_copy(which, k)
        copy.wait_recv()
        if mine is None:
            buf[k + 1] = buf[k] + land[k]
        else:
            mine(k + 1)
        copy.wait_send()
        if k + 1 < len(route):
            sum_copy(which, k + 1).start()

    big_sum, few_sum = (big, big_in, big_send, big_recv), (few, few_in, few_send, few_recv)

    def piece(jc, which):
        at = pl.multiple_of(jc * 8, 8) + (OFF - 4)
        for q in which:
            block = jnp.concatenate([ext[q * TR + k, pl.ds(at, 8), :] for k in range(2 * TR)], 0)
            turned = block.astype(BF16).T.astype(F32)
            patches[pl.ds(jc * (chans * step_rows) + q, chans, stride=step_rows), :] = turned

    def make_patches(which):
        def body(jc, carry):
            piece(jc, which)
            return carry

        lax.fori_loop(0, pieces - 1, body, 0, unroll=4)

    def patch_rows(c):
        def block(jc):
            return patches[pl.ds(jc * (chans * step_rows) + c * step_rows, bands), :]

        parts = []
        for jb in range(CHUNKS):
            parts.append(jnp.concatenate([block(2 * u + jb) for u in range(across)], 0).astype(BF16))
        return jnp.concatenate(parts, 1)

    def conv(which, first, last):
        width = CHUNKS * 16

        def channel(c, carry):
            base = master[c, which * width : (which + 1) * width, :]
            turned = [base] + [pltpu.roll(base, 32 * s, 1) for s in range(1, 4)]
            strips = [turned[p % 4] * masks[p * width : (p + 1) * width, :] for p in range(8)]
            weights = jnp.concatenate(
                [strips[p][16 * jb : 16 * jb + 16] for jb in range(CHUNKS) for p in range(8)], 0
            )
            y[pl.ds(pl.multiple_of(c * pitch, 8), tiles), :] = jnp.dot(
                patch_rows(c), weights, preferred_element_type=F32
            )
            return carry

        lax.fori_loop(first, last, channel, 0, unroll=16)

    start_rows(0)
    cot_load.start()

    def column(n, x):
        columns[n] = jnp.broadcast_to(x, (LANES, chans)).T

    width = CHUNKS * 16
    row_pitch = width + 8
    flat = jnp.concatenate([taps[a].astype(F32) for a in range(KS)] + [jnp.zeros((hot.shape[0] - KS * KS, chans), F32)], 0)
    flat = flat.astype(BF16).T

    def build_master(which):
        def some(i, carry):
            start = pl.multiple_of((which * width + 4 * i) * LANES, LANES)
            rows_of = jnp.dot(flat, hot[:, pl.ds(start, 4 * LANES)], preferred_element_type=F32)
            for k in range(4):
                y[pl.ds(4 * i + k, chans, stride=row_pitch), :] = rows_of[:, k * LANES : (k + 1) * LANES]
            return carry

        lax.fori_loop(0, width // 4, some, 0, unroll=4)

        def narrow(c, carry):
            at = pl.multiple_of(c * row_pitch, 8)
            master[c, which * width : (which + 1) * width, :] = y[pl.ds(at, width), :].astype(BF16)
            return carry

        lax.fori_loop(0, chans, narrow, 0, unroll=4)

    for n, x in enumerate((bias, gain, shift)):
        column(n, x[...])
    for n in range(hidden // chans):
        column(3 + n, b_in[:, n * chans : (n + 1) * chans])
    w_in_t[...] = w_in[...].T
    for m in range(rows + 2 * HALF, ext.shape[0]):
        ext[m] = jnp.zeros(ext.shape[1:], F32)
    build_master(0)
    for n in range(8):
        loads[n].wait()

        def fill(r, carry):
            ext[n * depth + r + HALF, OFF : OFF + cols, :] = out[n * depth + r].astype(F32)
            return carry

        lax.fori_loop(0, depth, fill, 0, unroll=2)
    make_patches(range(1, bands - 1))
    finish_rows(0)
    start_cols(0)
    build_master(1)
    make_patches((0, bands - 1))
    finish_cols(0)
    piece(0, range(bands))
    piece(pieces - 1, range(bands))
    conv(0, 0, chans)

    g_in[...] = jnp.zeros_like(g_in)
    g_out[...] = jnp.zeros_like(g_out)
    s_chan[...] = jnp.zeros_like(s_chan)
    s_bin[...] = jnp.zeros_like(s_bin)
    cot_load.wait()
    bias_rows, gain_rows, shift_rows = columns[0], columns[1], columns[2]

    def fold_lanes(x):
        total = x[:, :LANES]
        for k in range(1, bands):
            total = total + x[:, k * LANES : (k + 1) * LANES]
        return total

    def step(u, carry):
        t = u * bands
        nhats, rstds, parts = [], [], []
        for k in range(bands):
            yc = y[pl.ds(t + k, chans, stride=pitch), :] + bias_rows
            center = yc - jnp.sum(yc, 0, keepdims=True) * inv
            rstd = lax.rsqrt(jnp.sum(center * center, 0, keepdims=True) * inv + EPS)
            nhat = center * rstd
            nhats.append(nhat)
            rstds.append(rstd)
            parts.append((nhat * gain_rows + shift_rows).astype(BF16))
        normed = jnp.concatenate(parts, 1)
        start = pl.multiple_of(u * TC, TC)
        sea = blocks[0, u // per_block].astype(F32).astype(BF16)
        og = cot[:, pl.ds(start, TC), :].reshape(wide, chans) * sea
        pre_all = jnp.dot(w_in_t[...], normed, preferred_element_type=F32)
        dact_all = lax.dot_general(w_out[...], og, NT, preferred_element_type=F32)
        acts, dpres = [], []
        for r in range(0, hidden, STRIP):
            own = slice(r, r + STRIP)
            b_rows = columns[3 + r // chans, r % chans : r % chans + STRIP, :]
            pre = pre_all[own] + jnp.concatenate([b_rows] * bands, 1)
            square = pre * pre
            th = jnp.tanh(pre * (GELU_K + (GELU_K * GELU_C) * square))
            h = 0.5 + 0.5 * th
            act = pre * h
            slope = h + act * (1.0 - h) * (2.0 * GELU_K + (6.0 * GELU_K * GELU_C) * square)
            dpre = dact_all[own] * slope
            s_bin[own, :] += fold_lanes(dpre)
            acts.append(act.astype(BF16))
            dpres.append(dpre.astype(BF16))
        act_b, dpre_b = jnp.concatenate(acts, 0), jnp.concatenate(dpres, 0)
        g_out[...] += jnp.dot(act_b, og, preferred_element_type=F32)
        g_in[...] += lax.dot_general(normed, dpre_b, NT, preferred_element_type=F32)
        dnorm_all = jnp.dot(w_in[...], dpre_b, preferred_element_type=F32)
        sums = [None] * 3
        for k in range(bands):
            dnorm = dnorm_all[:, k * LANES : (k + 1) * LANES]
            nhat = nhats[k]
            scaled = dnorm * nhat
            dn = dnorm * gain_rows
            m1 = jnp.sum(dn, 0, keepdims=True) * inv
            m2 = jnp.sum(dn * nhat, 0, keepdims=True) * inv
            delta_b = (rstds[k] * (dn - m1 - nhat * m2)).astype(BF16)
            delta = delta_b.astype(F32)
            sums = [new if old is None else old + new for old, new in zip(sums, (scaled, dnorm, delta))]
            y[pl.ds(t + k, chans, stride=pitch), :] = delta
            ext[k * TR + HALF : (k + 1) * TR + HALF, pl.ds(start + OFF, TC), :] = (
                delta_b.T.astype(F32).reshape(TR, TC, chans)
            )
        for n in range(3):
            s_chan[n] += sums[n]
        return carry

    lax.fori_loop(0, across, step, 0)

    for m in range(HALF):
        edges[0, m] = ext[HALF + m, OFF : OFF + cols, :].astype(BF16)
        edges[1, m] = ext[rows + m, OFF : OFF + cols, :].astype(BF16)
    start_rows(1)
    in_share, out_share = chans // 2, hidden // 2
    dp = lax.axis_index("dp")

    def shares(at, k, land=None):
        wanted = (
            (0, g_in, pl.ds(pl.multiple_of(at * in_share, 8), in_share), slice(0, chans)),
            (in_share, g_in, pl.ds(pl.multiple_of(at * in_share, 8), in_share), slice(chans, 2 * chans)),
            (2 * in_share, g_out, pl.ds(pl.multiple_of(at * out_share, 8), out_share), slice(0, chans)),
        )
        for first, ref, some, lanes in wanted:
            to = slice(first, first + some.size)
            value = ref[some, lanes]
            big[k, to, :] = value if land is None else value + big_in[land, to, :]

    small = 2 * in_share + out_share
    shares(1 - dp, 0)
    rest = [jnp.sum(s_chan[n].T, 0, keepdims=True) for n in range(3)]
    rest += [jnp.sum(s_bin[n * chans : (n + 1) * chans, :].T, 0, keepdims=True) for n in range(2)]
    rest = jnp.concatenate(rest + [jnp.zeros((3, chans), F32)], 0)
    big[0, small : small + 8, :] = rest
    sum_copy(big_sum, 0).start()

    def first_sum(k):
        shares(dp, k, 0)
        to = slice(small, small + 8)
        big[k, to, :] = big[0, to, :] + big_in[0, to, :]

    def taps_of(first, last):
        def channel(c, carry):
            delta = y[pl.ds(pl.multiple_of(c * pitch, 8), tiles), :].astype(BF16)
            found = lax.dot_general(delta, patch_rows(c), TN, preferred_element_type=F32)
            for jb in range(2):
                acc = None
                for ro in range(TR):
                    term = None
                    for h in range(TC // 8):
                        at = ro * TC + 8 * h
                        some = found[at : at + 8, (jb + h) * LANES : (jb + h + 1) * LANES]
                        term = some if term is None else term + some
                    term = pltpu.roll(term, (LANES - 8 * ro) % LANES, 1) if ro else term
                    acc = term if acc is None else acc + term
                s_taps[jb, pl.ds(pl.multiple_of(c * 8, 8), 8), :] = acc
            return carry

        lax.fori_loop(first, last, channel, 0, unroll=16)

    taps_of(0, chans // 2)
    advance(big_sum, 0, first_sum)
    taps_of(chans // 2, chans)
    total = None
    for s in range(8):
        for jb in range(2):
            term = jnp.dot(
                s_taps[jb, pl.ds(s, chans, stride=8), :],
                gather[(2 * s + jb) * LANES : (2 * s + jb + 1) * LANES, :].astype(F32),
                precision=lax.Precision.HIGHEST,
                preferred_element_type=F32,
            )
            total = term if total is None else total + term
    few[0] = total.T[: few.shape[1]]
    sum_copy(few_sum, 0).start()
    advance(big_sum, 1)

    make_patches(range(1, bands - 1))
    finish_rows(1)
    start_cols(1)

    @pl.when(lat == top)
    def _():
        for m in range(HALF):
            fold[m] = ext[rows + HALF + m]
            ext[rows + HALF + m] = jnp.zeros(ext.shape[1:], F32)

    make_patches((0, bands - 1))
    advance(few_sum, 0)
    finish_cols(1)

    @pl.when(lat == top)
    def _():
        for side in (slice(0, OFF), slice(OFF + cols, 2 * OFF + cols)):
            for m in range(HALF):
                fold[m, side, :] = ext[rows + HALF + m, side, :]
                ext[rows + HALF + m, side, :] = jnp.zeros((OFF, chans), F32)

        def fold_step(i, carry):
            c0 = pl.multiple_of(i * TC, TC)
            for m in range(HALF):
                acc = jnp.zeros((TC, chans), F32)
                for n in range(m + 1):
                    a = KS - 1 - m + n
                    for b in range(KS):
                        v = fold[n, pl.ds(c0 + (OFF - HALF + b), TC), :]
                        acc = acc + v * taps[a, b : b + 1, :].astype(F32)
                folded[m, pl.ds(c0, TC), :] = acc
            return carry

        lax.fori_loop(0, across, fold_step, 0)

    @pl.when(lat < top)
    def _():
        folded[...] = jnp.zeros_like(folded)

    piece(0, range(bands))
    piece(pieces - 1, range(bands))
    advance(big_sum, 2)
    conv(1, 0, chans // 2)
    advance(few_sum, 1)
    conv(1, chans // 2, chans)
    advance(few_sum, 2)
    advance(big_sum, 3)

    def last_step(u, carry):
        at = pl.ds(pl.multiple_of(u * TC, TC), TC)
        for q in range(bands):
            direct = y[pl.ds(u * bands + q, chans, stride=pitch), :].T.reshape(TR, TC, chans)
            total = direct + cot[q * TR : (q + 1) * TR, at, :].astype(F32)
            if q == bands - 1:
                out[q * TR : rows - HALF, at, :] = total[: TR - HALF].astype(BF16)
                out[rows - HALF : rows, at, :] = (total[TR - HALF :] + folded[:, at, :]).astype(BF16)
            else:
                out[q * TR : (q + 1) * TR, at, :] = total.astype(BF16)
        return carry

    lax.fori_loop(0, across, last_step, 0)
    advance(few_sum, 3)
    for k in range(4, len(route)):
        advance(big_sum, k)
        advance(few_sum, k)
    totals[: small + 8, :] = big[len(route)]
    totals[small + 8 :, :] = few[len(route)]


def results_kernel(scale, grad, totals, out, o_in, o_out, o_taps, o_bias, o_gain, o_shift, o_bin, sems):
    rows = grad.shape[0]
    in_share, chans = o_in.shape[0], o_out.shape[1]
    small = 2 * in_share + o_out.shape[0]
    parts = sems.shape[0]
    depth = rows // parts
    copies = [
        pltpu.make_async_copy(grad.at[pl.ds(n * depth, depth)], out.at[pl.ds(n * depth, depth)], sems.at[n])
        for n in range(parts)
    ]
    for copy in copies:
        copy.start()
    o_in[:, :chans] = totals[:in_share, :] * scale
    o_in[:, chans:] = totals[in_share : 2 * in_share, :] * scale
    o_out[...] = totals[2 * in_share : small, :] * scale
    for n, ref in enumerate((o_gain, o_shift, o_bias)):
        ref[...] = totals[small + n : small + n + 1, :] * scale
    o_bin[:, :chans] = totals[small + 3 : small + 4, :] * scale
    o_bin[:, chans:] = totals[small + 4 : small + 5, :] * scale
    for a in range(KS):
        o_taps[a] = totals[small + 8 + a * KS : small + 8 + (a + 1) * KS, :] * scale
    for copy in copies:
        copy.wait()


def local(inputs, cotangent, kernel_dw, bias_dw, gain, shift_ln, w_in, b_in, w_out, ocean_mask):
    _, rows, cols, chans = inputs.shape
    hidden = w_in.shape[1]
    hot = spread()
    both = np.zeros((64, 2 * hot.shape[1]), np.float32)
    both[: KS * KS] = np.concatenate([hot, hot[::-1]], 1)
    bands, across = rows // TR, cols // TC
    tiles = bands * across
    steps = len(sum_route())
    shape = jax.ShapeDtypeStruct
    vmem = pl.BlockSpec(memory_space=pltpu.VMEM)
    smem = pl.BlockSpec(memory_space=pltpu.SMEM)
    far = pl.BlockSpec(memory_space=pl.ANY)
    groups = (rows + TR) // 4
    big_rows, few_rows = chans + hidden // 2 + 8, 56
    dma = pltpu.SemaphoreType.DMA
    grad, totals = pl.pallas_call(
        block_kernel,
        out_shape=(shape((rows, cols, chans), BF16), shape((big_rows + few_rows, chans), F32)),
        in_specs=[smem, far, far] + [vmem] * 10,
        out_specs=(vmem,) * 2,
        scratch_shapes=[
            pltpu.VMEM((rows + TR, cols + 2 * OFF, chans), F32),
            pltpu.VMEM(((cols // 8 + 1) * chans * (bands + 1), LANES), F32),
            pltpu.VMEM((chans * (tiles + 8), LANES), F32),
            pltpu.VMEM((rows, cols, chans), BF16),
            pltpu.VMEM((chans, 2 * CHUNKS * 16, LANES), BF16),
            pltpu.VMEM((3, chans, LANES), F32),
            pltpu.VMEM((hidden, LANES), F32),
            pltpu.VMEM((2, chans * 8, LANES), F32),
            pltpu.VMEM((chans, hidden), F32),
            pltpu.VMEM((hidden, chans), F32),
            pltpu.VMEM((3 + hidden // chans, chans, LANES), F32),
            pltpu.VMEM((hidden, chans), BF16),
            pltpu.VMEM((2, HALF, cols, chans), BF16),
            pltpu.VMEM((2, 2, HALF, cols, chans), BF16),
            pltpu.VMEM((2, 2, groups, 16, chans), BF16),
            pltpu.VMEM((2, 2, groups, 16, chans), BF16),
            pltpu.VMEM((HALF, cols + 2 * OFF, chans), F32),
            pltpu.VMEM((HALF, cols, chans), F32),
            pltpu.VMEM((steps + 1, big_rows, chans), F32),
            pltpu.VMEM((steps, big_rows, chans), F32),
            pltpu.VMEM((steps + 1, few_rows, chans), F32),
            pltpu.VMEM((steps, few_rows, chans), F32),
            dma((8,)), dma, dma((2, 5)), dma((2, 5)),
            dma((steps,)), dma((steps,)), dma((steps,)), dma((steps,)),
        ],
        compiler_params=pltpu.CompilerParams(
            collective_id=0, has_side_effects=True, vmem_limit_bytes=63 * 1024 * 1024
        ),
        cost_estimate=pl.CostEstimate(flops=20 << 30, bytes_accessed=12 << 20, transcendentals=4 << 20),
    )(
        ocean_mask, inputs[0], cotangent[0], jnp.asarray(both, BF16), jnp.asarray(row_masks(), BF16), kernel_dw, bias_dw[None],
        gain[None], shift_ln[None], w_in, b_in[None], w_out, jnp.asarray(gather_taps(), BF16),
    )
    cells_all = lax.axis_size("dp") * lax.axis_size("lat") * rows * lax.axis_size("lon") * cols
    grad, s_in, s_out, s_taps, s_bias, s_gain, s_shift, s_bin = pl.pallas_call(
        functools.partial(results_kernel, 1.0 / math.sqrt(cells_all)),
        out_shape=(
            shape((rows, cols, chans), BF16),
            shape((chans // 2, hidden), F32),
            shape((hidden // 2, chans), F32),
            shape((KS, KS, chans), F32),
            shape((1, chans), F32),
            shape((1, chans), F32),
            shape((1, chans), F32),
            shape((1, hidden), F32),
        ),
        in_specs=[far, vmem],
        out_specs=(far,) + (vmem,) * 7,
        scratch_shapes=[dma((8,))],
        compiler_params=pltpu.CompilerParams(vmem_limit_bytes=8 * 1024 * 1024),
    )(grad, totals)
    return grad[None], s_in, s_out, s_taps, s_bias[0], s_gain[0], s_shift[0], s_bin[0]


def solution(mesh):
    field = P(("groups", "dp"), "lat", "lon", None)
    placed = (field, field, P(), P(), P(), P(), P(), P(), P(), P("lat", "lon"))
    return jax.shard_map(
        local,
        mesh=mesh,
        in_specs=placed,
        out_specs=(
            field,
            P(("groups", "dp"), None),
            P(("groups", "dp"), None),
            P("groups", None, None),
            P("groups"),
            P("groups"),
            P("groups"),
            P("groups"),
        ),
        check_vma=False,
    )
```

```python
import functools
import math

import jax
import jax.numpy as jnp
import numpy as np
from jax import lax
from jax.experimental import pallas as pl
from jax.experimental.pallas import tpu as pltpu
from jax.sharding import PartitionSpec as P

KS = 7
HALF = 3
EPS = 1e-06
GELU_K = 0.7978845608
GELU_C = 0.044715
F32 = jnp.float32
BF16 = jnp.bfloat16
TR = 8
TC = 16
LANES = TR * TC
CHUNKS = TC // 8 + 1
DEPTH = CHUNKS * LANES
OFF = 8
SIDE = 4
MESH = pl.DeviceIdType.MESH
STRIP = 16
NT = (((1,), (1,)), ((), ()))
TN = (((0,), (0,)), ((), ()))


def spread():
    jb, ri, ji, ro, jo = np.meshgrid(*(np.arange(n) for n in (CHUNKS, 2, 8, TR, TC)), indexing="ij")
    a = (ri - ro) % 8
    b = 8 * jb + ji - jo - 1
    tap = np.where((a < KS) & (b >= 0) & (b < KS), a * KS + b, -1)
    hot = tap.reshape(1, -1) == np.arange(KS * KS)[:, None]
    return hot.astype(np.float32)


def row_masks():
    p, ri, ji, ro, jo = np.meshgrid(*(np.arange(n) for n in (4, 2, 8, TR, TC)), indexing="ij")
    low = (ro <= 2 * p + ri).reshape(4, 1, 16, LANES)
    both = np.concatenate([low, ~low], 0).astype(np.float32)
    return np.broadcast_to(both, (8, CHUNKS, 16, LANES)).reshape(8 * CHUNKS * 16, LANES)


def gather_taps():
    s, jb, ri, ji = np.meshgrid(*(np.arange(n) for n in (8, 2, 16, 8)), indexing="ij")
    b = 8 * jb + ji - s - 1
    tap = np.where((ri < KS) & (b >= 0) & (b < KS), ri * KS + b, -1)
    return (tap.reshape(-1, 1) == np.arange(LANES)[None]).astype(np.float32)


def frame_ids():
    lat, lats = lax.axis_index("lat"), lax.axis_size("lat")
    lon, lons = lax.axis_index("lon"), lax.axis_size("lon")
    return (
        {"lon": lax.rem(lon + lons - 1, lons)},
        {"lon": lax.rem(lon + 1, lons)},
        {"lat": jnp.minimum(lat + 1, lats - 1)},
        {"lat": jnp.maximum(lat - 1, 0)},
        {"lon": lons - 1 - lon},
    )


def sum_route():
    route = []
    for axis in ("dp", "lat", "lon"):
        step = 1
        while step < lax.axis_size(axis):
            route.append((axis, step))
            step *= 2
    return route


def partner(axis, step):
    at = lax.axis_index(axis)
    return {axis: at + step * (1 - 2 * ((at // step) % 2))}


def block_kernel(
    blocks, tile, cot_far, hot, masks, taps, bias, gain, shift, w_in, b_in, w_out, gather,
    grad, totals,
    out, ext, patches, y, cot, master, s_chan, s_bin, s_taps, g_in, g_out, columns, w_in_t,
    edges, rows_in, cols_in, packed, fold, folded, big, big_in, few, few_in,
    tile_sem, cot_sem, grad_sem, send_sem, recv_sem, big_send, big_recv, few_send, few_recv,
):
    rows, cols, chans = tile.shape
    hidden = w_out.shape[0]
    bands, across = rows // TR, cols // TC
    tiles = bands * across
    pitch = tiles + 8
    pieces = cols // 8 + 1
    step_rows = bands + 1
    wide = bands * LANES
    per_block = across // blocks.shape[1]
    lat, lats = lax.axis_index("lat"), lax.axis_size("lat")
    top = lats - 1
    west_of, east_of, above, below, mirror = frame_ids()
    route = sum_route()
    inv = 1.0 / chans

    depth = rows // 8
    loads = [
        pltpu.make_async_copy(tile.at[pl.ds(n * depth, depth)], out.at[pl.ds(n * depth, depth)], tile_sem.at[n])
        for n in range(8)
    ]
    for copy in loads:
        copy.start()
    cot_load = pltpu.make_async_copy(cot_far, cot, cot_sem)

    barrier = pltpu.get_barrier_semaphore()
    for device in (west_of, east_of):
        pl.semaphore_signal(barrier, inc=1, device_id=device, device_id_type=MESH)
    for axis, step in route:
        pl.semaphore_signal(barrier, inc=1, device_id=partner(axis, step), device_id_type=MESH)

    @pl.when(lat > 0)
    def _():
        pl.semaphore_signal(barrier, inc=1, device_id=below, device_id_type=MESH)

    @pl.when(lat < top)
    def _():
        pl.semaphore_signal(barrier, inc=1, device_id=above, device_id_type=MESH)

    @pl.when(lat == top)
    def _():
        pl.semaphore_signal(barrier, inc=1, device_id=mirror, device_id_type=MESH)

    pl.semaphore_wait(barrier, 3 + len(route) + jnp.minimum(lat, 1))

    def remote(source, target, sent, received, device):
        return pltpu.make_async_remote_copy(
            src_ref=source, dst_ref=target, send_sem=sent, recv_sem=received, device_id=device, device_id_type=MESH
        )

    def row_copies(n):
        if n:
            low, high = edges.at[0], edges.at[1]
        else:
            low, high = tile.at[pl.ds(0, HALF)], tile.at[pl.ds(rows - HALF, HALF)]
        sent, got = send_sem.at[n], recv_sem.at[n]
        return (
            (lat < top, remote(high, rows_in.at[n, 0], sent.at[0], got.at[0], above)),
            (lat > 0, remote(low, rows_in.at[n, 1], sent.at[1], got.at[1], below)),
            (lat == top, remote(high, rows_in.at[n, 1], sent.at[2], got.at[2], mirror)),
        )

    def start_rows(n):
        for wanted, copy in row_copies(n):
            pl.when(wanted)(copy.start)

    def finish_rows(n):
        (_, up), (_, down), (_, over) = row_copies(n)
        inside = slice(OFF, OFF + cols)

        @pl.when(lat > 0)
        def _():
            up.wait_recv()
            for m in range(HALF):
                ext[m, inside, :] = rows_in[n, 0, m].astype(F32)

        @pl.when(lat == 0)
        def _():
            for m in range(HALF):
                ext[m, inside, :] = jnp.zeros((cols, chans), F32)

        @pl.when(lat < top)
        def _():
            down.wait_recv()
            for m in range(HALF):
                ext[rows + HALF + m, inside, :] = rows_in[n, 1, m].astype(F32)

        @pl.when(lat == top)
        def _():
            over.wait_recv()
            shape = (cols, cols)
            swap = lax.broadcasted_iota(jnp.int32, shape, 0) + lax.broadcasted_iota(jnp.int32, shape, 1) == cols - 1
            swap = jnp.where(swap, 1.0, 0.0).astype(BF16)
            for m in range(HALF):
                ext[rows + HALF + m, inside, :] = jnp.dot(
                    swap, rows_in[n, 1, HALF - 1 - m], preferred_element_type=F32
                )

    def col_copies(n):
        sent, got = send_sem.at[n], recv_sem.at[n]
        return (
            remote(packed.at[n, 0], cols_in.at[n, 1], sent.at[3], got.at[3], west_of),
            remote(packed.at[n, 1], cols_in.at[n, 0], sent.at[4], got.at[4], east_of),
        )

    def start_cols(n):
        keep = lax.broadcasted_iota(jnp.int32, (8, chans), 0) < SIDE

        def pack(k, carry):
            for side, at in ((0, OFF), (1, OFF + cols - SIDE)):
                halves = []
                for m in range(0, 4, 2):
                    even = ext[4 * k + m, at : at + 8, :]
                    odd = ext[4 * k + m + 1, at - SIDE : at - SIDE + 8, :]
                    halves.append(jnp.where(keep, even, odd))
                packed[n, side, k] = jnp.concatenate(halves, 0).astype(BF16)
            return carry

        lax.fori_loop(0, packed.shape[2], pack, 0, unroll=6)
        for copy in col_copies(n):
            copy.start()

    def finish_cols(n):
        to_west, to_east = col_copies(n)
        to_west.wait_recv()
        to_east.wait_recv()

        def sides(k, carry):
            left, right = cols_in[n, 0, k].astype(F32), cols_in[n, 1, k].astype(F32)
            for m in range(4):
                ext[4 * k + m, OFF - SIDE : OFF, :] = left[SIDE * m : SIDE * m + SIDE]
                ext[4 * k + m, OFF + cols : OFF + cols + SIDE, :] = right[SIDE * m : SIDE * m + SIDE]
            return carry

        lax.fori_loop(0, packed.shape[2], sides, 0, unroll=6)
        to_west.wait_send()
        to_east.wait_send()
        for wanted, copy in row_copies(n):
            pl.when(wanted)(copy.wait_send)

    def sum_copy(few_or_big, k):
        buf, land, sent, got = few_or_big
        return remote(buf.at[k], land.at[k], sent.at[k], got.at[k], partner(*route[k]))

    def advance(which, k, mine=None):
        if k >= len(route):
            return
        buf, land = which[:2]
        copy = sum_copy(which, k)
        copy.wait_recv()
        if mine is None:
            buf[k + 1] = buf[k] + land[k]
        else:
            mine(k + 1)
        copy.wait_send()
        if k + 1 < len(route):
            sum_copy(which, k + 1).start()

    big_sum, few_sum = (big, big_in, big_send, big_recv), (few, few_in, few_send, few_recv)

    def piece(jc, which):
        at = pl.multiple_of(jc * 8, 8) + (OFF - 4)
        for q in which:
            block = jnp.concatenate([ext[q * TR + k, pl.ds(at, 8), :] for k in range(2 * TR)], 0)
            turned = block.astype(BF16).T.astype(F32)
            patches[pl.ds(jc * (chans * step_rows) + q, chans, stride=step_rows), :] = turned

    def make_patches(which):
        def body(jc, carry):
            piece(jc, which)
            return carry

        lax.fori_loop(0, pieces - 1, body, 0, unroll=4)

    def patch_rows(c):
        def block(jc):
            return patches[pl.ds(jc * (chans * step_rows) + c * step_rows, bands), :]

        parts = []
        for jb in range(CHUNKS):
            parts.append(jnp.concatenate([block(2 * u + jb) for u in range(across)], 0).astype(BF16))
        return jnp.concatenate(parts, 1)

    def conv(which, first, last):
        width = CHUNKS * 16

        def channel(c, carry):
            base = master[c, which * width : (which + 1) * width, :]
            turned = [base] + [pltpu.roll(base, 32 * s, 1) for s in range(1, 4)]
            strips = [turned[p % 4] * masks[p * width : (p + 1) * width, :] for p in range(8)]
            weights = jnp.concatenate(
                [strips[p][16 * jb : 16 * jb + 16] for jb in range(CHUNKS) for p in range(8)], 0
            )
            y[pl.ds(pl.multiple_of(c * pitch, 8), tiles), :] = jnp.dot(
                patch_rows(c), weights, preferred_element_type=F32
            )
            return carry

        lax.fori_loop(first, last, channel, 0, unroll=32)

    start_rows(0)
    cot_load.start()

    def column(n, x):
        columns[n] = jnp.broadcast_to(x, (LANES, chans)).T

    width = CHUNKS * 16
    row_pitch = width + 8
    flat = jnp.concatenate([taps[a].astype(F32) for a in range(KS)] + [jnp.zeros((hot.shape[0] - KS * KS, chans), F32)], 0)
    flat = flat.astype(BF16).T

    def build_master(which):
        def some(i, carry):
            start = pl.multiple_of((which * width + 4 * i) * LANES, LANES)
            rows_of = jnp.dot(flat, hot[:, pl.ds(start, 4 * LANES)], preferred_element_type=F32)
            for k in range(4):
                y[pl.ds(4 * i + k, chans, stride=row_pitch), :] = rows_of[:, k * LANES : (k + 1) * LANES]
            return carry

        lax.fori_loop(0, width // 4, some, 0, unroll=4)

        def narrow(c, carry):
            at = pl.multiple_of(c * row_pitch, 8)
            master[c, which * width : (which + 1) * width, :] = y[pl.ds(at, width), :].astype(BF16)
            return carry

        lax.fori_loop(0, chans, narrow, 0, unroll=4)

    for n, x in enumerate((bias, gain, shift)):
        column(n, x[...])
    for n in range(hidden // chans):
        column(3 + n, b_in[:, n * chans : (n + 1) * chans])
    w_in_t[...] = w_in[...].T
    for m in range(rows + 2 * HALF, ext.shape[0]):
        ext[m] = jnp.zeros(ext.shape[1:], F32)
    build_master(0)
    for n in range(8):
        loads[n].wait()

        def fill(r, carry):
            ext[n * depth + r + HALF, OFF : OFF + cols, :] = out[n * depth + r].astype(F32)
            return carry

        lax.fori_loop(0, depth, fill, 0, unroll=2)
    make_patches(range(1, bands - 1))
    finish_rows(0)
    start_cols(0)
    build_master(1)
    make_patches((0, bands - 1))
    finish_cols(0)
    piece(0, range(bands))
    piece(pieces - 1, range(bands))
    conv(0, 0, chans)

    g_in[...] = jnp.zeros_like(g_in)
    g_out[...] = jnp.zeros_like(g_out)
    s_chan[...] = jnp.zeros_like(s_chan)
    s_bin[...] = jnp.zeros_like(s_bin)
    cot_load.wait()
    bias_rows, gain_rows, shift_rows = columns[0], columns[1], columns[2]

    def step(u, carry):
        t = u * bands
        nhats, rstds, parts = [], [], []
        for k in range(bands):
            yc = y[pl.ds(t + k, chans, stride=pitch), :] + bias_rows
            center = yc - jnp.sum(yc, 0, keepdims=True) * inv
            rstd = lax.rsqrt(jnp.sum(center * center, 0, keepdims=True) * inv + EPS)
            nhat = center * rstd
            nhats.append(nhat)
            rstds.append(rstd)
            parts.append((nhat * gain_rows + shift_rows).astype(BF16))
        normed = jnp.concatenate(parts, 1)
        start = pl.multiple_of(u * TC, TC)
        sea = blocks[0, u // per_block].astype(F32).astype(BF16)
        og = cot[:, pl.ds(start, TC), :].reshape(wide, chans) * sea
        pre_all = jnp.dot(w_in_t[...], normed, preferred_element_type=F32)
        dact_all = lax.dot_general(w_out[...], og, NT, preferred_element_type=F32)
        acts, dpres = [], []
        for r in range(0, hidden, STRIP):
            own = slice(r, r + STRIP)
            b_rows = columns[3 + r // chans, r % chans : r % chans + STRIP, :]
            act_row, dpre_row, total = [], [], None
            for x in range(0, wide, 2 * LANES):
                cut = slice(x, x + 2 * LANES)
                pre = pre_all[own, cut] + jnp.concatenate([b_rows] * 2, 1)
                square = pre * pre
                th = jnp.tanh(pre * (GELU_K + (GELU_K * GELU_C) * square))
                h = 0.5 + 0.5 * th
                act = pre * h
                slope = h + act * (1.0 - h) * (2.0 * GELU_K + (6.0 * GELU_K * GELU_C) * square)
                dpre = dact_all[own, cut] * slope
                both = dpre[:, :LANES] + dpre[:, LANES:]
                total = both if total is None else total + both
                act_row.append(act.astype(BF16))
                dpre_row.append(dpre.astype(BF16))
            s_bin[own, :] += total
            acts.append(jnp.concatenate(act_row, 1))
            dpres.append(jnp.concatenate(dpre_row, 1))
        act_b, dpre_b = jnp.concatenate(acts, 0), jnp.concatenate(dpres, 0)
        g_out[...] += jnp.dot(act_b, og, preferred_element_type=F32)
        g_in[...] += lax.dot_general(normed, dpre_b, NT, preferred_element_type=F32)
        dnorm_all = jnp.dot(w_in[...], dpre_b, preferred_element_type=F32)
        sums = [None] * 3
        for k in range(bands):
            dnorm = dnorm_all[:, k * LANES : (k + 1) * LANES]
            nhat = nhats[k]
            scaled = dnorm * nhat
            dn = dnorm * gain_rows
            m1 = jnp.sum(dn, 0, keepdims=True) * inv
            m2 = jnp.sum(dn * nhat, 0, keepdims=True) * inv
            delta_b = (rstds[k] * (dn - m1 - nhat * m2)).astype(BF16)
            delta = delta_b.astype(F32)
            sums = [new if old is None else old + new for old, new in zip(sums, (scaled, dnorm, delta))]
            y[pl.ds(t + k, chans, stride=pitch), :] = delta
            ext[k * TR + HALF : (k + 1) * TR + HALF, pl.ds(start + OFF, TC), :] = (
                delta_b.T.astype(F32).reshape(TR, TC, chans)
            )
        for n in range(3):
            s_chan[n] += sums[n]
        return carry

    lax.fori_loop(0, across, step, 0)

    for m in range(HALF):
        edges[0, m] = ext[HALF + m, OFF : OFF + cols, :].astype(BF16)
        edges[1, m] = ext[rows + m, OFF : OFF + cols, :].astype(BF16)
    start_rows(1)
    in_share, out_share = chans // 2, hidden // 2
    dp = lax.axis_index("dp")

    def shares(at, k, land=None):
        wanted = (
            (0, g_in, pl.ds(pl.multiple_of(at * in_share, 8), in_share), slice(0, chans)),
            (in_share, g_in, pl.ds(pl.multiple_of(at * in_share, 8), in_share), slice(chans, 2 * chans)),
            (2 * in_share, g_out, pl.ds(pl.multiple_of(at * out_share, 8), out_share), slice(0, chans)),
        )
        for first, ref, some, lanes in wanted:
            to = slice(first, first + some.size)
            value = ref[some, lanes]
            big[k, to, :] = value if land is None else value + big_in[land, to, :]

    small = 2 * in_share + out_share
    shares(1 - dp, 0)
    rest = [jnp.sum(s_chan[n].T, 0, keepdims=True) for n in range(3)]
    rest += [jnp.sum(s_bin[n * chans : (n + 1) * chans, :].T, 0, keepdims=True) for n in range(2)]
    rest = jnp.concatenate(rest + [jnp.zeros((3, chans), F32)], 0)
    big[0, small : small + 8, :] = rest
    sum_copy(big_sum, 0).start()

    def first_sum(k):
        shares(dp, k, 0)
        to = slice(small, small + 8)
        big[k, to, :] = big[0, to, :] + big_in[0, to, :]

    def taps_of(first, last):
        def channel(c, carry):
            delta = y[pl.ds(pl.multiple_of(c * pitch, 8), tiles), :].astype(BF16)
            found = lax.dot_general(delta, patch_rows(c), TN, preferred_element_type=F32)
            for jb in range(2):
                acc = None
                for ro in range(TR):
                    term = None
                    for h in range(TC // 8):
                        at = ro * TC + 8 * h
                        some = found[at : at + 8, (jb + h) * LANES : (jb + h + 1) * LANES]
                        term = some if term is None else term + some
                    term = pltpu.roll(term, (LANES - 8 * ro) % LANES, 1) if ro else term
                    acc = term if acc is None else acc + term
                s_taps[jb, pl.ds(pl.multiple_of(c * 8, 8), 8), :] = acc
            return carry

        lax.fori_loop(first, last, channel, 0, unroll=16)

    taps_of(0, chans // 2)
    advance(big_sum, 0, first_sum)
    taps_of(chans // 2, chans)
    total = None
    for s in range(8):
        for jb in range(2):
            term = jnp.dot(
                s_taps[jb, pl.ds(s, chans, stride=8), :],
                gather[(2 * s + jb) * LANES : (2 * s + jb + 1) * LANES, :].astype(F32),
                precision=lax.Precision.HIGHEST,
                preferred_element_type=F32,
            )
            total = term if total is None else total + term
    few[0] = total.T[: few.shape[1]]
    sum_copy(few_sum, 0).start()
    make_patches(range(1, bands - 1))
    finish_rows(1)
    start_cols(1)

    @pl.when(lat == top)
    def _():
        for m in range(HALF):
            fold[m] = ext[rows + HALF + m]
            ext[rows + HALF + m] = jnp.zeros(ext.shape[1:], F32)

    make_patches((0, bands - 1))
    advance(few_sum, 0)
    finish_cols(1)
    advance(big_sum, 1)

    @pl.when(lat == top)
    def _():
        for side in (slice(0, OFF), slice(OFF + cols, 2 * OFF + cols)):
            for m in range(HALF):
                fold[m, side, :] = ext[rows + HALF + m, side, :]
                ext[rows + HALF + m, side, :] = jnp.zeros((OFF, chans), F32)

        def fold_step(i, carry):
            c0 = pl.multiple_of(i * TC, TC)
            for m in range(HALF):
                acc = jnp.zeros((TC, chans), F32)
                for n in range(m + 1):
                    a = KS - 1 - m + n
                    for b in range(KS):
                        v = fold[n, pl.ds(c0 + (OFF - HALF + b), TC), :]
                        acc = acc + v * taps[a, b : b + 1, :].astype(F32)
                folded[m, pl.ds(c0, TC), :] = acc
            return carry

        lax.fori_loop(0, across, fold_step, 0, unroll=4)

    @pl.when(lat < top)
    def _():
        folded[...] = jnp.zeros_like(folded)

    piece(0, range(bands))
    piece(pieces - 1, range(bands))
    conv(1, 0, chans // 2)
    advance(big_sum, 2)
    advance(few_sum, 1)
    conv(1, chans // 2, chans)
    advance(few_sum, 2)

    def last_step(u, carry):
        at = pl.ds(pl.multiple_of(u * TC, TC), TC)
        for q in range(bands):
            direct = y[pl.ds(u * bands + q, chans, stride=pitch), :].T.reshape(TR, TC, chans)
            total = direct + cot[q * TR : (q + 1) * TR, at, :].astype(F32)
            if q == bands - 1:
                out[q * TR : rows - HALF, at, :] = total[: TR - HALF].astype(BF16)
                out[rows - HALF : rows, at, :] = (total[TR - HALF :] + folded[:, at, :]).astype(BF16)
            else:
                out[q * TR : (q + 1) * TR, at, :] = total.astype(BF16)
        return carry

    parts = grad_sem.shape[0]
    writes = []
    for n in range(parts):
        lax.fori_loop(n * across // parts, (n + 1) * across // parts, last_step, 0)
        at = pl.ds(n * cols // parts, cols // parts)
        writes.append(pltpu.make_async_copy(out.at[:, at], grad.at[:, at], grad_sem.at[n]))
        writes[n].start()
    advance(big_sum, 3)
    advance(few_sum, 3)
    for k in range(4, len(route)):
        advance(big_sum, k)
        advance(few_sum, k)
    totals[: small + 8, :] = big[len(route)]
    totals[small + 8 :, :] = few[len(route)]
    for copy in writes:
        copy.wait()


def results_kernel(
    scale, grad, totals, out, o_in, o_out, o_taps, o_bias, o_gain, o_shift, o_bin, held, come, gone
):
    rows = grad.shape[0]
    in_share, chans = o_in.shape[0], o_out.shape[1]
    small = 2 * in_share + o_out.shape[0]
    parts = come.shape[0]
    depth = rows // parts
    spans = [pl.ds(n * depth, depth) for n in range(parts)]
    reads = [pltpu.make_async_copy(grad.at[at], held.at[at], come.at[n]) for n, at in enumerate(spans)]
    writes = [pltpu.make_async_copy(held.at[at], out.at[at], gone.at[n]) for n, at in enumerate(spans)]
    for copy in reads:
        copy.start()
    for n in range(parts):
        reads[n].wait()
        writes[n].start()
    o_in[:, :chans] = totals[:in_share, :] * scale
    o_in[:, chans:] = totals[in_share : 2 * in_share, :] * scale
    o_out[...] = totals[2 * in_share : small, :] * scale
    for n, ref in enumerate((o_gain, o_shift, o_bias)):
        ref[...] = totals[small + n : small + n + 1, :] * scale
    o_bin[:, :chans] = totals[small + 3 : small + 4, :] * scale
    o_bin[:, chans:] = totals[small + 4 : small + 5, :] * scale
    for a in range(KS):
        o_taps[a] = totals[small + 8 + a * KS : small + 8 + (a + 1) * KS, :] * scale
    for copy in writes:
        copy.wait()


def local(inputs, cotangent, kernel_dw, bias_dw, gain, shift_ln, w_in, b_in, w_out, ocean_mask):
    _, rows, cols, chans = inputs.shape
    hidden = w_in.shape[1]
    hot = spread()
    both = np.zeros((64, 2 * hot.shape[1]), np.float32)
    both[: KS * KS] = np.concatenate([hot, hot[::-1]], 1)
    bands, across = rows // TR, cols // TC
    tiles = bands * across
    steps = len(sum_route())
    shape = jax.ShapeDtypeStruct
    vmem = pl.BlockSpec(memory_space=pltpu.VMEM)
    smem = pl.BlockSpec(memory_space=pltpu.SMEM)
    far = pl.BlockSpec(memory_space=pl.ANY)
    groups = (rows + TR) // 4
    big_rows, few_rows = chans + hidden // 2 + 8, 56
    dma = pltpu.SemaphoreType.DMA
    grad, totals = pl.pallas_call(
        block_kernel,
        out_shape=(shape((rows, cols, chans), BF16), shape((big_rows + few_rows, chans), F32)),
        in_specs=[smem, far, far] + [vmem] * 10,
        out_specs=(far, vmem),
        scratch_shapes=[
            pltpu.VMEM((rows, cols, chans), BF16),
            pltpu.VMEM((rows + TR, cols + 2 * OFF, chans), F32),
            pltpu.VMEM(((cols // 8 + 1) * chans * (bands + 1), LANES), F32),
            pltpu.VMEM((chans * (tiles + 8), LANES), F32),
            pltpu.VMEM((rows, cols, chans), BF16),
            pltpu.VMEM((chans, 2 * CHUNKS * 16, LANES), BF16),
            pltpu.VMEM((3, chans, LANES), F32),
            pltpu.VMEM((hidden, LANES), F32),
            pltpu.VMEM((2, chans * 8, LANES), F32),
            pltpu.VMEM((chans, hidden), F32),
            pltpu.VMEM((hidden, chans), F32),
            pltpu.VMEM((3 + hidden // chans, chans, LANES), F32),
            pltpu.VMEM((hidden, chans), BF16),
            pltpu.VMEM((2, HALF, cols, chans), BF16),
            pltpu.VMEM((2, 2, HALF, cols, chans), BF16),
            pltpu.VMEM((2, 2, groups, 16, chans), BF16),
            pltpu.VMEM((2, 2, groups, 16, chans), BF16),
            pltpu.VMEM((HALF, cols + 2 * OFF, chans), F32),
            pltpu.VMEM((HALF, cols, chans), F32),
            pltpu.VMEM((steps + 1, big_rows, chans), F32),
            pltpu.VMEM((steps, big_rows, chans), F32),
            pltpu.VMEM((steps + 1, few_rows, chans), F32),
            pltpu.VMEM((steps, few_rows, chans), F32),
            dma((8,)), dma, dma((4,)), dma((2, 5)), dma((2, 5)),
            dma((steps,)), dma((steps,)), dma((steps,)), dma((steps,)),
        ],
        compiler_params=pltpu.CompilerParams(
            collective_id=0, has_side_effects=True, vmem_limit_bytes=63 * 1024 * 1024
        ),
        cost_estimate=pl.CostEstimate(flops=20 << 30, bytes_accessed=12 << 20, transcendentals=4 << 20),
    )(
        ocean_mask, inputs[0], cotangent[0], jnp.asarray(both, BF16), jnp.asarray(row_masks(), BF16), kernel_dw, bias_dw[None],
        gain[None], shift_ln[None], w_in, b_in[None], w_out, jnp.asarray(gather_taps(), BF16),
    )
    cells_all = lax.axis_size("dp") * lax.axis_size("lat") * rows * lax.axis_size("lon") * cols
    grad, s_in, s_out, s_taps, s_bias, s_gain, s_shift, s_bin = pl.pallas_call(
        functools.partial(results_kernel, 1.0 / math.sqrt(cells_all)),
        out_shape=(
            shape((rows, cols, chans), BF16),
            shape((chans // 2, hidden), F32),
            shape((hidden // 2, chans), F32),
            shape((KS, KS, chans), F32),
            shape((1, chans), F32),
            shape((1, chans), F32),
            shape((1, chans), F32),
            shape((1, hidden), F32),
        ),
        in_specs=[far, vmem],
        out_specs=(far,) + (vmem,) * 7,
        scratch_shapes=[pltpu.VMEM((rows, cols, chans), BF16), dma((8,)), dma((8,))],
        compiler_params=pltpu.CompilerParams(vmem_limit_bytes=60 * 1024 * 1024),
    )(grad, totals)
    return grad[None], s_in, s_out, s_taps, s_bias[0], s_gain[0], s_shift[0], s_bin[0]


def solution(mesh):
    field = P(("groups", "dp"), "lat", "lon", None)
    placed = (field, field, P(), P(), P(), P(), P(), P(), P(), P("lat", "lon"))
    return jax.shard_map(
        local,
        mesh=mesh,
        in_specs=placed,
        out_specs=(
            field,
            P(("groups", "dp"), None),
            P(("groups", "dp"), None),
            P("groups", None, None),
            P("groups"),
            P("groups"),
            P("groups"),
            P("groups"),
        ),
        check_vma=False,
    )
```

```python
import functools
import math

import jax
import jax.numpy as jnp
import numpy as np
from jax import lax
from jax.experimental import pallas as pl
from jax.experimental.pallas import tpu as pltpu
from jax.sharding import PartitionSpec as P

KS = 7
HALF = 3
EPS = 1e-06
GELU_K = 0.7978845608
GELU_C = 0.044715
F32 = jnp.float32
BF16 = jnp.bfloat16
TR = 8
TC = 16
LANES = TR * TC
CHUNKS = TC // 8 + 1
DEPTH = CHUNKS * LANES
OFF = 8
SIDE = 4
MESH = pl.DeviceIdType.MESH
STRIP = 16
NT = (((1,), (1,)), ((), ()))
TN = (((0,), (0,)), ((), ()))


def spread():
    jb, ri, ji, ro, jo = np.meshgrid(*(np.arange(n) for n in (CHUNKS, 2, 8, TR, TC)), indexing="ij")
    a = (ri - ro) % 8
    b = 8 * jb + ji - jo - 1
    tap = np.where((a < KS) & (b >= 0) & (b < KS), a * KS + b, -1)
    hot = tap.reshape(1, -1) == np.arange(KS * KS)[:, None]
    return hot.astype(np.float32)


def row_masks():
    p, ri, ji, ro, jo = np.meshgrid(*(np.arange(n) for n in (4, 2, 8, TR, TC)), indexing="ij")
    low = (ro <= 2 * p + ri).reshape(4, 1, 16, LANES)
    both = np.concatenate([low, ~low], 0).astype(np.float32)
    return np.broadcast_to(both, (8, CHUNKS, 16, LANES)).reshape(8 * CHUNKS * 16, LANES)


def gather_taps():
    s, jb, ri, ji = np.meshgrid(*(np.arange(n) for n in (8, 2, 16, 8)), indexing="ij")
    b = 8 * jb + ji - s - 1
    tap = np.where((ri < KS) & (b >= 0) & (b < KS), ri * KS + b, -1)
    return (tap.reshape(-1, 1) == np.arange(LANES)[None]).astype(np.float32)


def frame_ids():
    lat, lats = lax.axis_index("lat"), lax.axis_size("lat")
    lon, lons = lax.axis_index("lon"), lax.axis_size("lon")
    return (
        {"lon": lax.rem(lon + lons - 1, lons)},
        {"lon": lax.rem(lon + 1, lons)},
        {"lat": jnp.minimum(lat + 1, lats - 1)},
        {"lat": jnp.maximum(lat - 1, 0)},
        {"lon": lons - 1 - lon},
    )


def sum_route():
    route = []
    for axis in ("dp", "lat", "lon"):
        step = 1
        while step < lax.axis_size(axis):
            route.append((axis, step))
            step *= 2
    return route


def partner(axis, step):
    at = lax.axis_index(axis)
    return {axis: at + step * (1 - 2 * ((at // step) % 2))}


def block_kernel(
    blocks, tile, cot_far, hot_far, masks, taps, bias, gain, shift, w_in, b_in, w_out, gather_far,
    grad, totals,
    out, hot, gather, ext, patches, y, cot, master, s_chan, s_bin, s_taps, g_in, g_out, columns, w_in_t,
    edges, rows_in, cols_in, packed, fold, folded, big, big_in, few, few_in,
    tile_sem, cot_sem, hot_sem, gather_sem, grad_sem, send_sem, recv_sem, big_send, big_recv, few_send, few_recv,
):
    rows, cols, chans = tile.shape
    hidden = w_out.shape[0]
    bands, across = rows // TR, cols // TC
    tiles = bands * across
    pitch = tiles + 8
    pieces = cols // 8 + 1
    step_rows = bands + 1
    wide = bands * LANES
    per_block = across // blocks.shape[1]
    lat, lats = lax.axis_index("lat"), lax.axis_size("lat")
    top = lats - 1
    west_of, east_of, above, below, mirror = frame_ids()
    route = sum_route()
    inv = 1.0 / chans

    depth = rows // 8
    loads = [
        pltpu.make_async_copy(tile.at[pl.ds(n * depth, depth)], out.at[pl.ds(n * depth, depth)], tile_sem.at[n])
        for n in range(8)
    ]
    hot_load = pltpu.make_async_copy(hot_far, hot, hot_sem)
    gather_load = pltpu.make_async_copy(gather_far, gather, gather_sem)
    hot_load.start()
    for copy in loads:
        copy.start()
    cot_load = pltpu.make_async_copy(cot_far, cot, cot_sem)

    barrier = pltpu.get_barrier_semaphore()
    for device in (west_of, east_of):
        pl.semaphore_signal(barrier, inc=1, device_id=device, device_id_type=MESH)
    for axis, step in route:
        pl.semaphore_signal(barrier, inc=1, device_id=partner(axis, step), device_id_type=MESH)

    @pl.when(lat > 0)
    def _():
        pl.semaphore_signal(barrier, inc=1, device_id=below, device_id_type=MESH)

    @pl.when(lat < top)
    def _():
        pl.semaphore_signal(barrier, inc=1, device_id=above, device_id_type=MESH)

    @pl.when(lat == top)
    def _():
        pl.semaphore_signal(barrier, inc=1, device_id=mirror, device_id_type=MESH)

    pl.semaphore_wait(barrier, 3 + len(route) + jnp.minimum(lat, 1))

    def remote(source, target, sent, received, device):
        return pltpu.make_async_remote_copy(
            src_ref=source, dst_ref=target, send_sem=sent, recv_sem=received, device_id=device, device_id_type=MESH
        )

    def row_copies(n):
        if n:
            low, high = edges.at[0], edges.at[1]
        else:
            low, high = tile.at[pl.ds(0, HALF)], tile.at[pl.ds(rows - HALF, HALF)]
        sent, got = send_sem.at[n], recv_sem.at[n]
        return (
            (lat < top, remote(high, rows_in.at[n, 0], sent.at[0], got.at[0], above)),
            (lat > 0, remote(low, rows_in.at[n, 1], sent.at[1], got.at[1], below)),
            (lat == top, remote(high, rows_in.at[n, 1], sent.at[2], got.at[2], mirror)),
        )

    def start_rows(n):
        for wanted, copy in row_copies(n):
            pl.when(wanted)(copy.start)

    def finish_rows(n):
        (_, up), (_, down), (_, over) = row_copies(n)
        inside = slice(OFF, OFF + cols)

        @pl.when(lat > 0)
        def _():
            up.wait_recv()
            for m in range(HALF):
                ext[m, inside, :] = rows_in[n, 0, m].astype(F32)

        @pl.when(lat == 0)
        def _():
            for m in range(HALF):
                ext[m, inside, :] = jnp.zeros((cols, chans), F32)

        @pl.when(lat < top)
        def _():
            down.wait_recv()
            for m in range(HALF):
                ext[rows + HALF + m, inside, :] = rows_in[n, 1, m].astype(F32)

        @pl.when(lat == top)
        def _():
            over.wait_recv()
            shape = (cols, cols)
            swap = lax.broadcasted_iota(jnp.int32, shape, 0) + lax.broadcasted_iota(jnp.int32, shape, 1) == cols - 1
            swap = jnp.where(swap, 1.0, 0.0).astype(BF16)
            for m in range(HALF):
                ext[rows + HALF + m, inside, :] = jnp.dot(
                    swap, rows_in[n, 1, HALF - 1 - m], preferred_element_type=F32
                )

    def col_copies(n):
        sent, got = send_sem.at[n], recv_sem.at[n]
        return (
            remote(packed.at[n, 0], cols_in.at[n, 1], sent.at[3], got.at[3], west_of),
            remote(packed.at[n, 1], cols_in.at[n, 0], sent.at[4], got.at[4], east_of),
        )

    def start_cols(n):
        keep = lax.broadcasted_iota(jnp.int32, (8, chans), 0) < SIDE

        def pack(k, carry):
            for side, at in ((0, OFF), (1, OFF + cols - SIDE)):
                halves = []
                for m in range(0, 4, 2):
                    even = ext[4 * k + m, at : at + 8, :]
                    odd = ext[4 * k + m + 1, at - SIDE : at - SIDE + 8, :]
                    halves.append(jnp.where(keep, even, odd))
                packed[n, side, k] = jnp.concatenate(halves, 0).astype(BF16)
            return carry

        lax.fori_loop(0, packed.shape[2], pack, 0, unroll=6)
        for copy in col_copies(n):
            copy.start()

    def finish_cols(n):
        to_west, to_east = col_copies(n)
        to_west.wait_recv()
        to_east.wait_recv()

        def sides(k, carry):
            left, right = cols_in[n, 0, k].astype(F32), cols_in[n, 1, k].astype(F32)
            for m in range(4):
                ext[4 * k + m, OFF - SIDE : OFF, :] = left[SIDE * m : SIDE * m + SIDE]
                ext[4 * k + m, OFF + cols : OFF + cols + SIDE, :] = right[SIDE * m : SIDE * m + SIDE]
            return carry

        lax.fori_loop(0, packed.shape[2], sides, 0, unroll=6)
        to_west.wait_send()
        to_east.wait_send()
        for wanted, copy in row_copies(n):
            pl.when(wanted)(copy.wait_send)

    def sum_copy(few_or_big, k):
        buf, land, sent, got = few_or_big
        return remote(buf.at[k], land.at[k], sent.at[k], got.at[k], partner(*route[k]))

    def advance(which, k, mine=None):
        if k >= len(route):
            return
        buf, land = which[:2]
        copy = sum_copy(which, k)
        copy.wait_recv()
        if mine is None:
            buf[k + 1] = buf[k] + land[k]
        else:
            mine(k + 1)
        copy.wait_send()
        if k + 1 < len(route):
            sum_copy(which, k + 1).start()

    big_sum, few_sum = (big, big_in, big_send, big_recv), (few, few_in, few_send, few_recv)

    def piece(jc, which):
        at = pl.multiple_of(jc * 8, 8) + (OFF - 4)
        for q in which:
            block = jnp.concatenate([ext[q * TR + k, pl.ds(at, 8), :] for k in range(2 * TR)], 0)
            turned = block.astype(BF16).T.astype(F32)
            patches[pl.ds(jc * (chans * step_rows) + q, chans, stride=step_rows), :] = turned

    def make_patches(which):
        def body(jc, carry):
            piece(jc, which)
            return carry

        lax.fori_loop(0, pieces - 1, body, 0, unroll=4)

    def patch_rows(c):
        def block(jc):
            return patches[pl.ds(jc * (chans * step_rows) + c * step_rows, bands), :]

        parts = []
        for jb in range(CHUNKS):
            parts.append(jnp.concatenate([block(2 * u + jb) for u in range(across)], 0).astype(BF16))
        return jnp.concatenate(parts, 1)

    def conv(which, first, last):
        width = CHUNKS * 16

        def channel(c, carry):
            base = master[c, which * width : (which + 1) * width, :]
            turned = [base] + [pltpu.roll(base, 32 * s, 1) for s in range(1, 4)]
            strips = [turned[p % 4] * masks[p * width : (p + 1) * width, :] for p in range(8)]
            weights = jnp.concatenate(
                [strips[p][16 * jb : 16 * jb + 16] for jb in range(CHUNKS) for p in range(8)], 0
            )
            y[pl.ds(pl.multiple_of(c * pitch, 8), tiles), :] = jnp.dot(
                patch_rows(c), weights, preferred_element_type=F32
            )
            return carry

        lax.fori_loop(first, last, channel, 0, unroll=32)

    start_rows(0)
    cot_load.start()
    gather_load.start()

    def column(n, x):
        columns[n] = jnp.broadcast_to(x, (LANES, chans)).T

    width = CHUNKS * 16
    row_pitch = width + 8
    flat = jnp.concatenate([taps[a].astype(F32) for a in range(KS)] + [jnp.zeros((hot.shape[0] - KS * KS, chans), F32)], 0)
    flat = flat.astype(BF16).T

    def build_master(which):
        def some(i, carry):
            start = pl.multiple_of((which * width + 4 * i) * LANES, LANES)
            rows_of = jnp.dot(flat, hot[:, pl.ds(start, 4 * LANES)], preferred_element_type=F32)
            for k in range(4):
                y[pl.ds(4 * i + k, chans, stride=row_pitch), :] = rows_of[:, k * LANES : (k + 1) * LANES]
            return carry

        lax.fori_loop(0, width // 4, some, 0, unroll=4)

        def narrow(c, carry):
            at = pl.multiple_of(c * row_pitch, 8)
            master[c, which * width : (which + 1) * width, :] = y[pl.ds(at, width), :].astype(BF16)
            return carry

        lax.fori_loop(0, chans, narrow, 0, unroll=4)

    for n, x in enumerate((bias, gain, shift)):
        column(n, x[...])
    for n in range(hidden // chans):
        column(3 + n, b_in[:, n * chans : (n + 1) * chans])
    w_in_t[...] = w_in[...].T
    for m in range(rows + 2 * HALF, ext.shape[0]):
        ext[m] = jnp.zeros(ext.shape[1:], F32)
    hot_load.wait()
    build_master(0)
    for n in range(8):
        loads[n].wait()

        def fill(r, carry):
            ext[n * depth + r + HALF, OFF : OFF + cols, :] = out[n * depth + r].astype(F32)
            return carry

        lax.fori_loop(0, depth, fill, 0, unroll=2)
    make_patches(range(1, bands - 1))
    finish_rows(0)
    start_cols(0)
    build_master(1)
    make_patches((0, bands - 1))
    finish_cols(0)
    piece(0, range(bands))
    piece(pieces - 1, range(bands))
    conv(0, 0, chans)

    g_in[...] = jnp.zeros_like(g_in)
    g_out[...] = jnp.zeros_like(g_out)
    s_chan[...] = jnp.zeros_like(s_chan)
    s_bin[...] = jnp.zeros_like(s_bin)
    cot_load.wait()
    gather_load.wait()
    bias_rows, gain_rows, shift_rows = columns[0], columns[1], columns[2]

    def step(u, carry):
        t = u * bands
        nhats, rstds, parts = [], [], []
        for k in range(bands):
            yc = y[pl.ds(t + k, chans, stride=pitch), :] + bias_rows
            center = yc - jnp.sum(yc, 0, keepdims=True) * inv
            rstd = lax.rsqrt(jnp.sum(center * center, 0, keepdims=True) * inv + EPS)
            nhat = center * rstd
            nhats.append(nhat)
            rstds.append(rstd)
            parts.append((nhat * gain_rows + shift_rows).astype(BF16))
        normed = jnp.concatenate(parts, 1)
        start = pl.multiple_of(u * TC, TC)
        sea = blocks[0, u // per_block].astype(F32).astype(BF16)
        og = cot[:, pl.ds(start, TC), :].reshape(wide, chans) * sea
        pre_all = jnp.dot(w_in_t[...], normed, preferred_element_type=F32)
        dact_all = lax.dot_general(w_out[...], og, NT, preferred_element_type=F32)
        acts, dpres = [], []
        for r in range(0, hidden, STRIP):
            own = slice(r, r + STRIP)
            b_rows = columns[3 + r // chans, r % chans : r % chans + STRIP, :]
            act_row, dpre_row, total = [], [], None
            for x in range(0, wide, 2 * LANES):
                cut = slice(x, x + 2 * LANES)
                pre = pre_all[own, cut] + jnp.concatenate([b_rows] * 2, 1)
                square = pre * pre
                th = jnp.tanh(pre * (GELU_K + (GELU_K * GELU_C) * square))
                h = 0.5 + 0.5 * th
                act = pre * h
                slope = h + act * (1.0 - h) * (2.0 * GELU_K + (6.0 * GELU_K * GELU_C) * square)
                dpre = dact_all[own, cut] * slope
                both = dpre[:, :LANES] + dpre[:, LANES:]
                total = both if total is None else total + both
                act_row.append(act.astype(BF16))
                dpre_row.append(dpre.astype(BF16))
            s_bin[own, :] += total
            acts.append(jnp.concatenate(act_row, 1))
            dpres.append(jnp.concatenate(dpre_row, 1))
        act_b, dpre_b = jnp.concatenate(acts, 0), jnp.concatenate(dpres, 0)
        g_out[...] += jnp.dot(act_b, og, preferred_element_type=F32)
        g_in[...] += lax.dot_general(normed, dpre_b, NT, preferred_element_type=F32)
        dnorm_all = jnp.dot(w_in[...], dpre_b, preferred_element_type=F32)
        sums = [None] * 3
        for k in range(bands):
            dnorm = dnorm_all[:, k * LANES : (k + 1) * LANES]
            nhat = nhats[k]
            scaled = dnorm * nhat
            dn = dnorm * gain_rows
            m1 = jnp.sum(dn, 0, keepdims=True) * inv
            m2 = jnp.sum(dn * nhat, 0, keepdims=True) * inv
            delta_b = (rstds[k] * (dn - m1 - nhat * m2)).astype(BF16)
            delta = delta_b.astype(F32)
            sums = [new if old is None else old + new for old, new in zip(sums, (scaled, dnorm, delta))]
            y[pl.ds(t + k, chans, stride=pitch), :] = delta
            ext[k * TR + HALF : (k + 1) * TR + HALF, pl.ds(start + OFF, TC), :] = (
                delta_b.T.astype(F32).reshape(TR, TC, chans)
            )
        for n in range(3):
            s_chan[n] += sums[n]
        return carry

    lax.fori_loop(0, across, step, 0)

    for m in range(HALF):
        edges[0, m] = ext[HALF + m, OFF : OFF + cols, :].astype(BF16)
        edges[1, m] = ext[rows + m, OFF : OFF + cols, :].astype(BF16)
    start_rows(1)
    in_share, out_share = chans // 2, hidden // 2
    dp = lax.axis_index("dp")

    def shares(at, k, land=None):
        wanted = (
            (0, g_in, pl.ds(pl.multiple_of(at * in_share, 8), in_share), slice(0, chans)),
            (in_share, g_in, pl.ds(pl.multiple_of(at * in_share, 8), in_share), slice(chans, 2 * chans)),
            (2 * in_share, g_out, pl.ds(pl.multiple_of(at * out_share, 8), out_share), slice(0, chans)),
        )
        for first, ref, some, lanes in wanted:
            to = slice(first, first + some.size)
            value = ref[some, lanes]
            big[k, to, :] = value if land is None else value + big_in[land, to, :]

    small = 2 * in_share + out_share
    shares(1 - dp, 0)
    rest = [jnp.sum(s_chan[n].T, 0, keepdims=True) for n in range(3)]
    rest += [jnp.sum(s_bin[n * chans : (n + 1) * chans, :].T, 0, keepdims=True) for n in range(2)]
    rest = jnp.concatenate(rest + [jnp.zeros((3, chans), F32)], 0)
    big[0, small : small + 8, :] = rest
    sum_copy(big_sum, 0).start()

    def first_sum(k):
        shares(dp, k, 0)
        to = slice(small, small + 8)
        big[k, to, :] = big[0, to, :] + big_in[0, to, :]

    def taps_of(first, last):
        def channel(c, carry):
            delta = y[pl.ds(pl.multiple_of(c * pitch, 8), tiles), :].astype(BF16)
            found = lax.dot_general(delta, patch_rows(c), TN, preferred_element_type=F32)
            for jb in range(2):
                acc = None
                for ro in range(TR):
                    term = None
                    for h in range(TC // 8):
                        at = ro * TC + 8 * h
                        some = found[at : at + 8, (jb + h) * LANES : (jb + h + 1) * LANES]
                        term = some if term is None else term + some
                    term = pltpu.roll(term, (LANES - 8 * ro) % LANES, 1) if ro else term
                    acc = term if acc is None else acc + term
                s_taps[jb, pl.ds(pl.multiple_of(c * 8, 8), 8), :] = acc
            return carry

        lax.fori_loop(first, last, channel, 0, unroll=16)

    taps_of(0, chans // 2)
    advance(big_sum, 0, first_sum)
    taps_of(chans // 2, chans)
    total = None
    for s in range(8):
        for jb in range(2):
            term = jnp.dot(
                s_taps[jb, pl.ds(s, chans, stride=8), :],
                gather[(2 * s + jb) * LANES : (2 * s + jb + 1) * LANES, :].astype(F32),
                precision=lax.Precision.HIGHEST,
                preferred_element_type=F32,
            )
            total = term if total is None else total + term
    few[0] = total.T[: few.shape[1]]
    sum_copy(few_sum, 0).start()
    make_patches(range(1, bands - 1))
    finish_rows(1)
    start_cols(1)

    @pl.when(lat == top)
    def _():
        for m in range(HALF):
            fold[m] = ext[rows + HALF + m]
            ext[rows + HALF + m] = jnp.zeros(ext.shape[1:], F32)

    make_patches((0, bands - 1))
    advance(few_sum, 0)
    finish_cols(1)
    advance(big_sum, 1)

    @pl.when(lat == top)
    def _():
        for side in (slice(0, OFF), slice(OFF + cols, 2 * OFF + cols)):
            for m in range(HALF):
                fold[m, side, :] = ext[rows + HALF + m, side, :]
                ext[rows + HALF + m, side, :] = jnp.zeros((OFF, chans), F32)

        def fold_step(i, carry):
            c0 = pl.multiple_of(i * TC, TC)
            for m in range(HALF):
                acc = jnp.zeros((TC, chans), F32)
                for n in range(m + 1):
                    a = KS - 1 - m + n
                    for b in range(KS):
                        v = fold[n, pl.ds(c0 + (OFF - HALF + b), TC), :]
                        acc = acc + v * taps[a, b : b + 1, :].astype(F32)
                folded[m, pl.ds(c0, TC), :] = acc
            return carry

        lax.fori_loop(0, across, fold_step, 0, unroll=4)

    @pl.when(lat < top)
    def _():
        folded[...] = jnp.zeros_like(folded)

    piece(0, range(bands))
    piece(pieces - 1, range(bands))
    conv(1, 0, chans // 2)
    advance(big_sum, 2)
    advance(few_sum, 1)
    conv(1, chans // 2, chans)
    advance(few_sum, 2)

    def last_step(u, carry):
        at = pl.ds(pl.multiple_of(u * TC, TC), TC)
        for q in range(bands):
            direct = y[pl.ds(u * bands + q, chans, stride=pitch), :].T.reshape(TR, TC, chans)
            total = direct + cot[q * TR : (q + 1) * TR, at, :].astype(F32)
            if q == bands - 1:
                out[q * TR : rows - HALF, at, :] = total[: TR - HALF].astype(BF16)
                out[rows - HALF : rows, at, :] = (total[TR - HALF :] + folded[:, at, :]).astype(BF16)
            else:
                out[q * TR : (q + 1) * TR, at, :] = total.astype(BF16)
        return carry

    parts = grad_sem.shape[0]
    writes = []
    for n in range(parts):
        lax.fori_loop(n * across // parts, (n + 1) * across // parts, last_step, 0)
        at = pl.ds(n * cols // parts, cols // parts)
        writes.append(pltpu.make_async_copy(out.at[:, at], grad.at[:, at], grad_sem.at[n]))
        writes[n].start()
    advance(big_sum, 3)
    advance(few_sum, 3)
    for k in range(4, len(route)):
        advance(big_sum, k)
        advance(few_sum, k)
    totals[: small + 8, :] = big[len(route)]
    totals[small + 8 :, :] = few[len(route)]
    for copy in writes:
        copy.wait()


def results_kernel(
    scale, grad, totals, out, o_in, o_out, o_taps, o_bias, o_gain, o_shift, o_bin, held, come, gone
):
    rows = grad.shape[0]
    in_share, chans = o_in.shape[0], o_out.shape[1]
    small = 2 * in_share + o_out.shape[0]
    parts = come.shape[0]
    depth = rows // parts
    spans = [pl.ds(n * depth, depth) for n in range(parts)]
    reads = [pltpu.make_async_copy(grad.at[at], held.at[at], come.at[n]) for n, at in enumerate(spans)]
    writes = [pltpu.make_async_copy(held.at[at], out.at[at], gone.at[n]) for n, at in enumerate(spans)]
    for copy in reads:
        copy.start()
    for n in range(parts):
        reads[n].wait()
        writes[n].start()
    o_in[:, :chans] = totals[:in_share, :] * scale
    o_in[:, chans:] = totals[in_share : 2 * in_share, :] * scale
    o_out[...] = totals[2 * in_share : small, :] * scale
    for n, ref in enumerate((o_gain, o_shift, o_bias)):
        ref[...] = totals[small + n : small + n + 1, :] * scale
    o_bin[:, :chans] = totals[small + 3 : small + 4, :] * scale
    o_bin[:, chans:] = totals[small + 4 : small + 5, :] * scale
    for a in range(KS):
        o_taps[a] = totals[small + 8 + a * KS : small + 8 + (a + 1) * KS, :] * scale
    for copy in writes:
        copy.wait()


def local(inputs, cotangent, kernel_dw, bias_dw, gain, shift_ln, w_in, b_in, w_out, ocean_mask):
    _, rows, cols, chans = inputs.shape
    hidden = w_in.shape[1]
    hot = spread()
    both = np.zeros((64, 2 * hot.shape[1]), np.float32)
    both[: KS * KS] = np.concatenate([hot, hot[::-1]], 1)
    bands, across = rows // TR, cols // TC
    tiles = bands * across
    steps = len(sum_route())
    shape = jax.ShapeDtypeStruct
    vmem = pl.BlockSpec(memory_space=pltpu.VMEM)
    smem = pl.BlockSpec(memory_space=pltpu.SMEM)
    far = pl.BlockSpec(memory_space=pl.ANY)
    groups = (rows + TR) // 4
    big_rows, few_rows = chans + hidden // 2 + 8, 56
    dma = pltpu.SemaphoreType.DMA
    grad, totals = pl.pallas_call(
        block_kernel,
        out_shape=(shape((rows, cols, chans), BF16), shape((big_rows + few_rows, chans), F32)),
        in_specs=[smem, far, far, far] + [vmem] * 8 + [far],
        out_specs=(far, vmem),
        scratch_shapes=[
            pltpu.VMEM((rows, cols, chans), BF16),
            pltpu.VMEM(both.shape, BF16),
            pltpu.VMEM(gather_taps().shape, BF16),
            pltpu.VMEM((rows + TR, cols + 2 * OFF, chans), F32),
            pltpu.VMEM(((cols // 8 + 1) * chans * (bands + 1), LANES), F32),
            pltpu.VMEM((chans * (tiles + 8), LANES), F32),
            pltpu.VMEM((rows, cols, chans), BF16),
            pltpu.VMEM((chans, 2 * CHUNKS * 16, LANES), BF16),
            pltpu.VMEM((3, chans, LANES), F32),
            pltpu.VMEM((hidden, LANES), F32),
            pltpu.VMEM((2, chans * 8, LANES), F32),
            pltpu.VMEM((chans, hidden), F32),
            pltpu.VMEM((hidden, chans), F32),
            pltpu.VMEM((3 + hidden // chans, chans, LANES), F32),
            pltpu.VMEM((hidden, chans), BF16),
            pltpu.VMEM((2, HALF, cols, chans), BF16),
            pltpu.VMEM((2, 2, HALF, cols, chans), BF16),
            pltpu.VMEM((2, 2, groups, 16, chans), BF16),
            pltpu.VMEM((2, 2, groups, 16, chans), BF16),
            pltpu.VMEM((HALF, cols + 2 * OFF, chans), F32),
            pltpu.VMEM((HALF, cols, chans), F32),
            pltpu.VMEM((steps + 1, big_rows, chans), F32),
            pltpu.VMEM((steps, big_rows, chans), F32),
            pltpu.VMEM((steps + 1, few_rows, chans), F32),
            pltpu.VMEM((steps, few_rows, chans), F32),
            dma((8,)), dma, dma, dma, dma((4,)), dma((2, 5)), dma((2, 5)),
            dma((steps,)), dma((steps,)), dma((steps,)), dma((steps,)),
        ],
        compiler_params=pltpu.CompilerParams(
            collective_id=0, has_side_effects=True, vmem_limit_bytes=63 * 1024 * 1024
        ),
        cost_estimate=pl.CostEstimate(flops=20 << 30, bytes_accessed=12 << 20, transcendentals=4 << 20),
    )(
        ocean_mask, inputs[0], cotangent[0], jnp.asarray(both, BF16), jnp.asarray(row_masks(), BF16), kernel_dw, bias_dw[None],
        gain[None], shift_ln[None], w_in, b_in[None], w_out, jnp.asarray(gather_taps(), BF16),
    )
    cells_all = lax.axis_size("dp") * lax.axis_size("lat") * rows * lax.axis_size("lon") * cols
    grad, s_in, s_out, s_taps, s_bias, s_gain, s_shift, s_bin = pl.pallas_call(
        functools.partial(results_kernel, 1.0 / math.sqrt(cells_all)),
        out_shape=(
            shape((rows, cols, chans), BF16),
            shape((chans // 2, hidden), F32),
            shape((hidden // 2, chans), F32),
            shape((KS, KS, chans), F32),
            shape((1, chans), F32),
            shape((1, chans), F32),
            shape((1, chans), F32),
            shape((1, hidden), F32),
        ),
        in_specs=[far, vmem],
        out_specs=(far,) + (vmem,) * 7,
        scratch_shapes=[pltpu.VMEM((rows, cols, chans), BF16), dma((8,)), dma((8,))],
        compiler_params=pltpu.CompilerParams(vmem_limit_bytes=60 * 1024 * 1024),
    )(grad, totals)
    return grad[None], s_in, s_out, s_taps, s_bias[0], s_gain[0], s_shift[0], s_bin[0]


def solution(mesh):
    field = P(("groups", "dp"), "lat", "lon", None)
    placed = (field, field, P(), P(), P(), P(), P(), P(), P(), P("lat", "lon"))
    return jax.shard_map(
        local,
        mesh=mesh,
        in_specs=placed,
        out_specs=(
            field,
            P(("groups", "dp"), None),
            P(("groups", "dp"), None),
            P("groups", None, None),
            P("groups"),
            P("groups"),
            P("groups"),
            P("groups"),
        ),
        check_vma=False,
    )
```

```python
import functools
import math

import jax
import jax.numpy as jnp
import numpy as np
from jax import lax
from jax.experimental import pallas as pl
from jax.experimental.pallas import tpu as pltpu
from jax.sharding import PartitionSpec as P

KS = 7
HALF = 3
EPS = 1e-06
GELU_K = 0.7978845608
GELU_C = 0.044715
F32 = jnp.float32
BF16 = jnp.bfloat16
TR = 8
TC = 16
LANES = TR * TC
CHUNKS = TC // 8 + 1
DEPTH = CHUNKS * LANES
OFF = 8
SIDE = 4
MESH = pl.DeviceIdType.MESH
STRIP = 16
NT = (((1,), (1,)), ((), ()))
TN = (((0,), (0,)), ((), ()))


def spread():
    jb, ri, ji, ro, jo = np.meshgrid(*(np.arange(n) for n in (CHUNKS, 2, 8, TR, TC)), indexing="ij")
    a = (ri - ro) % 8
    b = 8 * jb + ji - jo - 1
    tap = np.where((a < KS) & (b >= 0) & (b < KS), a * KS + b, -1)
    hot = tap.reshape(1, -1) == np.arange(KS * KS)[:, None]
    return hot.astype(np.float32)


def row_masks():
    p, ri, ji, ro, jo = np.meshgrid(*(np.arange(n) for n in (4, 2, 8, TR, TC)), indexing="ij")
    low = (ro <= 2 * p + ri).reshape(4, 1, 16, LANES)
    both = np.concatenate([low, ~low], 0).astype(np.float32)
    return np.broadcast_to(both, (8, CHUNKS, 16, LANES)).reshape(8 * CHUNKS * 16, LANES)


def gather_taps():
    s, jb, ri, ji = np.meshgrid(*(np.arange(n) for n in (8, 2, 16, 8)), indexing="ij")
    b = 8 * jb + ji - s - 1
    tap = np.where((ri < KS) & (b >= 0) & (b < KS), ri * KS + b, -1)
    return (tap.reshape(-1, 1) == np.arange(LANES)[None]).astype(np.float32)


def frame_ids():
    lat, lats = lax.axis_index("lat"), lax.axis_size("lat")
    lon, lons = lax.axis_index("lon"), lax.axis_size("lon")
    return (
        {"lon": lax.rem(lon + lons - 1, lons)},
        {"lon": lax.rem(lon + 1, lons)},
        {"lat": jnp.minimum(lat + 1, lats - 1)},
        {"lat": jnp.maximum(lat - 1, 0)},
        {"lon": lons - 1 - lon},
    )


def sum_route():
    route = []
    for axis in ("dp", "lat", "lon"):
        step = 1
        while step < lax.axis_size(axis):
            route.append((axis, step))
            step *= 2
    return route


def partner(axis, step):
    at = lax.axis_index(axis)
    return {axis: at + step * (1 - 2 * ((at // step) % 2))}


def block_kernel(
    blocks, tile, cot_far, hot_far, masks, taps, bias, gain, shift, w_in, b_in, w_out, gather_far,
    grad, totals,
    out, hot, gather, ext, patches, y, cot, master, s_chan, s_bin, s_taps, g_in, g_out, columns, w_in_t,
    edges, rows_in, cols_in, packed, fold, folded, big, big_in, few, few_in,
    tile_sem, cot_sem, hot_sem, gather_sem, grad_sem, send_sem, recv_sem, big_send, big_recv, few_send, few_recv,
):
    rows, cols, chans = tile.shape
    hidden = w_out.shape[0]
    bands, across = rows // TR, cols // TC
    tiles = bands * across
    pitch = tiles + 8
    pieces = cols // 8 + 1
    step_rows = bands + 1
    wide = bands * LANES
    per_block = across // blocks.shape[1]
    lat, lats = lax.axis_index("lat"), lax.axis_size("lat")
    top = lats - 1
    west_of, east_of, above, below, mirror = frame_ids()
    route = sum_route()
    inv = 1.0 / chans

    depth = rows // 8
    loads = [
        pltpu.make_async_copy(tile.at[pl.ds(n * depth, depth)], out.at[pl.ds(n * depth, depth)], tile_sem.at[n])
        for n in range(8)
    ]
    hot_load = pltpu.make_async_copy(hot_far, hot, hot_sem)
    gather_load = pltpu.make_async_copy(gather_far, gather, gather_sem)
    hot_load.start()
    for copy in loads:
        copy.start()
    cot_load = pltpu.make_async_copy(cot_far, cot, cot_sem)

    barrier = pltpu.get_barrier_semaphore()
    for device in (west_of, east_of):
        pl.semaphore_signal(barrier, inc=1, device_id=device, device_id_type=MESH)
    for axis, step in route:
        pl.semaphore_signal(barrier, inc=1, device_id=partner(axis, step), device_id_type=MESH)

    @pl.when(lat > 0)
    def _():
        pl.semaphore_signal(barrier, inc=1, device_id=below, device_id_type=MESH)

    @pl.when(lat < top)
    def _():
        pl.semaphore_signal(barrier, inc=1, device_id=above, device_id_type=MESH)

    @pl.when(lat == top)
    def _():
        pl.semaphore_signal(barrier, inc=1, device_id=mirror, device_id_type=MESH)

    pl.semaphore_wait(barrier, 3 + len(route) + jnp.minimum(lat, 1))

    def remote(source, target, sent, received, device):
        return pltpu.make_async_remote_copy(
            src_ref=source, dst_ref=target, send_sem=sent, recv_sem=received, device_id=device, device_id_type=MESH
        )

    def row_copies(n):
        if n:
            low, high = edges.at[0], edges.at[1]
        else:
            low, high = tile.at[pl.ds(0, HALF)], tile.at[pl.ds(rows - HALF, HALF)]
        sent, got = send_sem.at[n], recv_sem.at[n]
        return (
            (lat < top, remote(high, rows_in.at[n, 0], sent.at[0], got.at[0], above)),
            (lat > 0, remote(low, rows_in.at[n, 1], sent.at[1], got.at[1], below)),
            (lat == top, remote(high, rows_in.at[n, 1], sent.at[2], got.at[2], mirror)),
        )

    def start_rows(n):
        for wanted, copy in row_copies(n):
            pl.when(wanted)(copy.start)

    def finish_rows(n):
        (_, up), (_, down), (_, over) = row_copies(n)
        inside = slice(OFF, OFF + cols)

        @pl.when(lat > 0)
        def _():
            up.wait_recv()
            for m in range(HALF):
                ext[m, inside, :] = rows_in[n, 0, m].astype(F32)

        @pl.when(lat == 0)
        def _():
            for m in range(HALF):
                ext[m, inside, :] = jnp.zeros((cols, chans), F32)

        @pl.when(lat < top)
        def _():
            down.wait_recv()
            for m in range(HALF):
                ext[rows + HALF + m, inside, :] = rows_in[n, 1, m].astype(F32)

        @pl.when(lat == top)
        def _():
            over.wait_recv()
            shape = (cols, cols)
            swap = lax.broadcasted_iota(jnp.int32, shape, 0) + lax.broadcasted_iota(jnp.int32, shape, 1) == cols - 1
            swap = jnp.where(swap, 1.0, 0.0).astype(BF16)
            for m in range(HALF):
                ext[rows + HALF + m, inside, :] = jnp.dot(
                    swap, rows_in[n, 1, HALF - 1 - m], preferred_element_type=F32
                )

    def col_copies(n):
        sent, got = send_sem.at[n], recv_sem.at[n]
        return (
            remote(packed.at[n, 0], cols_in.at[n, 1], sent.at[3], got.at[3], west_of),
            remote(packed.at[n, 1], cols_in.at[n, 0], sent.at[4], got.at[4], east_of),
        )

    def start_cols(n):
        keep = lax.broadcasted_iota(jnp.int32, (8, chans), 0) < SIDE

        def pack(k, carry):
            for side, at in ((0, OFF), (1, OFF + cols - SIDE)):
                halves = []
                for m in range(0, 4, 2):
                    even = ext[4 * k + m, at : at + 8, :]
                    odd = ext[4 * k + m + 1, at - SIDE : at - SIDE + 8, :]
                    halves.append(jnp.where(keep, even, odd))
                packed[n, side, k] = jnp.concatenate(halves, 0).astype(BF16)
            return carry

        lax.fori_loop(0, packed.shape[2], pack, 0, unroll=6)
        for copy in col_copies(n):
            copy.start()

    def finish_cols(n):
        to_west, to_east = col_copies(n)
        to_west.wait_recv()
        to_east.wait_recv()

        def sides(k, carry):
            left, right = cols_in[n, 0, k].astype(F32), cols_in[n, 1, k].astype(F32)
            for m in range(4):
                ext[4 * k + m, OFF - SIDE : OFF, :] = left[SIDE * m : SIDE * m + SIDE]
                ext[4 * k + m, OFF + cols : OFF + cols + SIDE, :] = right[SIDE * m : SIDE * m + SIDE]
            return carry

        lax.fori_loop(0, packed.shape[2], sides, 0, unroll=6)
        to_west.wait_send()
        to_east.wait_send()
        for wanted, copy in row_copies(n):
            pl.when(wanted)(copy.wait_send)

    def sum_copy(few_or_big, k):
        buf, land, sent, got = few_or_big
        return remote(buf.at[k], land.at[k], sent.at[k], got.at[k], partner(*route[k]))

    def advance(which, k, mine=None):
        if k >= len(route):
            return
        buf, land = which[:2]
        copy = sum_copy(which, k)
        copy.wait_recv()
        if mine is None:
            buf[k + 1] = buf[k] + land[k]
        else:
            mine(k + 1)
        copy.wait_send()
        if k + 1 < len(route):
            sum_copy(which, k + 1).start()

    big_sum, few_sum = (big, big_in, big_send, big_recv), (few, few_in, few_send, few_recv)

    def piece(jc, which):
        at = pl.multiple_of(jc * 8, 8) + (OFF - 4)
        for q in which:
            block = jnp.concatenate([ext[q * TR + k, pl.ds(at, 8), :] for k in range(2 * TR)], 0)
            turned = block.astype(BF16).T.astype(F32)
            patches[pl.ds(jc * (chans * step_rows) + q, chans, stride=step_rows), :] = turned

    def make_patches(which):
        def body(jc, carry):
            piece(jc, which)
            return carry

        lax.fori_loop(0, pieces - 1, body, 0, unroll=4)

    def patch_rows(c):
        def block(jc):
            return patches[pl.ds(jc * (chans * step_rows) + c * step_rows, bands), :]

        parts = []
        for jb in range(CHUNKS):
            parts.append(jnp.concatenate([block(2 * u + jb) for u in range(across)], 0).astype(BF16))
        return jnp.concatenate(parts, 1)

    def conv(which, first, last):
        width = CHUNKS * 16

        def channel(c, carry):
            base = master[c, which * width : (which + 1) * width, :]
            turned = [base] + [pltpu.roll(base, 32 * s, 1) for s in range(1, 4)]
            strips = [turned[p % 4] * masks[p * width : (p + 1) * width, :] for p in range(8)]
            weights = jnp.concatenate(
                [strips[p][16 * jb : 16 * jb + 16] for jb in range(CHUNKS) for p in range(8)], 0
            )
            y[pl.ds(pl.multiple_of(c * pitch, 8), tiles), :] = jnp.dot(
                patch_rows(c), weights, preferred_element_type=F32
            )
            return carry

        lax.fori_loop(first, last, channel, 0, unroll=32)

    start_rows(0)
    cot_load.start()
    gather_load.start()

    def column(n, x):
        columns[n] = jnp.broadcast_to(x, (LANES, chans)).T

    width = CHUNKS * 16
    row_pitch = width + 8
    flat = jnp.concatenate([taps[a].astype(F32) for a in range(KS)] + [jnp.zeros((hot.shape[0] - KS * KS, chans), F32)], 0)
    flat = flat.astype(BF16).T

    def build_master(which):
        def some(i, carry):
            start = pl.multiple_of((which * width + 4 * i) * LANES, LANES)
            rows_of = jnp.dot(flat, hot[:, pl.ds(start, 4 * LANES)], preferred_element_type=F32)
            for k in range(4):
                y[pl.ds(4 * i + k, chans, stride=row_pitch), :] = rows_of[:, k * LANES : (k + 1) * LANES]
            return carry

        lax.fori_loop(0, width // 4, some, 0, unroll=4)

        def narrow(c, carry):
            at = pl.multiple_of(c * row_pitch, 8)
            master[c, which * width : (which + 1) * width, :] = y[pl.ds(at, width), :].astype(BF16)
            return carry

        lax.fori_loop(0, chans, narrow, 0, unroll=4)

    for n, x in enumerate((bias, gain, shift)):
        column(n, x[...])
    for n in range(hidden // chans):
        column(3 + n, b_in[:, n * chans : (n + 1) * chans])
    w_in_t[...] = w_in[...].T
    for m in range(rows + 2 * HALF, ext.shape[0]):
        ext[m] = jnp.zeros(ext.shape[1:], F32)
    hot_load.wait()
    build_master(0)
    for n in range(8):
        loads[n].wait()

        def fill(r, carry):
            ext[n * depth + r + HALF, OFF : OFF + cols, :] = out[n * depth + r].astype(F32)
            return carry

        lax.fori_loop(0, depth, fill, 0, unroll=2)
    make_patches(range(1, bands - 1))
    finish_rows(0)
    start_cols(0)
    build_master(1)
    make_patches((0, bands - 1))
    finish_cols(0)
    piece(0, range(bands))
    piece(pieces - 1, range(bands))
    conv(0, 0, chans)

    g_in[...] = jnp.zeros_like(g_in)
    g_out[...] = jnp.zeros_like(g_out)
    s_chan[...] = jnp.zeros_like(s_chan)
    s_bin[...] = jnp.zeros_like(s_bin)
    cot_load.wait()
    gather_load.wait()
    bias_rows, gain_rows, shift_rows = columns[0], columns[1], columns[2]

    def step(u, carry):
        t = u * bands
        nhats, rstds, parts = [], [], []
        for k in range(bands):
            yc = y[pl.ds(t + k, chans, stride=pitch), :] + bias_rows
            center = yc - jnp.sum(yc, 0, keepdims=True) * inv
            rstd = lax.rsqrt(jnp.sum(center * center, 0, keepdims=True) * inv + EPS)
            nhat = center * rstd
            nhats.append(nhat)
            rstds.append(rstd)
            parts.append((nhat * gain_rows + shift_rows).astype(BF16))
        normed = jnp.concatenate(parts, 1)
        start = pl.multiple_of(u * TC, TC)
        sea = blocks[0, u // per_block].astype(F32).astype(BF16)
        og = cot[:, pl.ds(start, TC), :].reshape(wide, chans) * sea
        pre_all = jnp.dot(w_in_t[...], normed, preferred_element_type=F32)
        dact_all = lax.dot_general(w_out[...], og, NT, preferred_element_type=F32)
        acts, dpres = [], []
        for r in range(0, hidden, STRIP):
            own = slice(r, r + STRIP)
            b_rows = columns[3 + r // chans, r % chans : r % chans + STRIP, :]
            act_row, dpre_row, total = [], [], None
            for x in range(0, wide, 2 * LANES):
                cut = slice(x, x + 2 * LANES)
                pre = pre_all[own, cut] + jnp.concatenate([b_rows] * 2, 1)
                square = pre * pre
                th = jnp.tanh(pre * (GELU_K + (GELU_K * GELU_C) * square))
                h = 0.5 + 0.5 * th
                act = pre * h
                slope = h + act * (1.0 - h) * (2.0 * GELU_K + (6.0 * GELU_K * GELU_C) * square)
                dpre = dact_all[own, cut] * slope
                both = dpre[:, :LANES] + dpre[:, LANES:]
                total = both if total is None else total + both
                act_row.append(act.astype(BF16))
                dpre_row.append(dpre.astype(BF16))
            s_bin[own, :] += total
            acts.append(jnp.concatenate(act_row, 1))
            dpres.append(jnp.concatenate(dpre_row, 1))
        act_b, dpre_b = jnp.concatenate(acts, 0), jnp.concatenate(dpres, 0)
        g_out[...] += jnp.dot(act_b, og, preferred_element_type=F32)
        g_in[...] += lax.dot_general(normed, dpre_b, NT, preferred_element_type=F32)
        dnorm_all = jnp.dot(w_in[...], dpre_b, preferred_element_type=F32)
        sums = [None] * 3
        for k in range(bands):
            dnorm = dnorm_all[:, k * LANES : (k + 1) * LANES]
            nhat = nhats[k]
            scaled = dnorm * nhat
            dn = dnorm * gain_rows
            m1 = jnp.sum(dn, 0, keepdims=True) * inv
            m2 = jnp.sum(dn * nhat, 0, keepdims=True) * inv
            delta_b = (rstds[k] * (dn - m1 - nhat * m2)).astype(BF16)
            delta = delta_b.astype(F32)
            sums = [new if old is None else old + new for old, new in zip(sums, (scaled, dnorm, delta))]
            y[pl.ds(t + k, chans, stride=pitch), :] = delta
            ext[k * TR + HALF : (k + 1) * TR + HALF, pl.ds(start + OFF, TC), :] = (
                delta_b.T.astype(F32).reshape(TR, TC, chans)
            )
        for n in range(3):
            s_chan[n] += sums[n]
        return carry

    lax.fori_loop(0, across, step, 0)

    for m in range(HALF):
        edges[0, m] = ext[HALF + m, OFF : OFF + cols, :].astype(BF16)
        edges[1, m] = ext[rows + m, OFF : OFF + cols, :].astype(BF16)
    start_rows(1)
    in_share, out_share = chans // 2, hidden // 2
    dp = lax.axis_index("dp")

    def shares(at, k, land=None):
        wanted = (
            (0, g_in, pl.ds(pl.multiple_of(at * in_share, 8), in_share), slice(0, chans)),
            (in_share, g_in, pl.ds(pl.multiple_of(at * in_share, 8), in_share), slice(chans, 2 * chans)),
            (2 * in_share, g_out, pl.ds(pl.multiple_of(at * out_share, 8), out_share), slice(0, chans)),
        )
        for first, ref, some, lanes in wanted:
            to = slice(first, first + some.size)
            value = ref[some, lanes]
            big[k, to, :] = value if land is None else value + big_in[land, to, :]

    small = 2 * in_share + out_share
    shares(1 - dp, 0)
    rest = [jnp.sum(s_chan[n].T, 0, keepdims=True) for n in range(3)]
    rest += [jnp.sum(s_bin[n * chans : (n + 1) * chans, :].T, 0, keepdims=True) for n in range(2)]
    rest = jnp.concatenate(rest + [jnp.zeros((3, chans), F32)], 0)
    big[0, small : small + 8, :] = rest
    sum_copy(big_sum, 0).start()

    def first_sum(k):
        shares(dp, k, 0)
        to = slice(small, small + 8)
        big[k, to, :] = big[0, to, :] + big_in[0, to, :]

    def taps_of(first, last):
        def channel(c, carry):
            delta = y[pl.ds(pl.multiple_of(c * pitch, 8), tiles), :].astype(BF16)
            found = lax.dot_general(delta, patch_rows(c), TN, preferred_element_type=F32)
            for jb in range(2):
                acc = None
                for ro in range(TR):
                    term = None
                    for h in range(TC // 8):
                        at = ro * TC + 8 * h
                        some = found[at : at + 8, (jb + h) * LANES : (jb + h + 1) * LANES]
                        term = some if term is None else term + some
                    term = pltpu.roll(term, (LANES - 8 * ro) % LANES, 1) if ro else term
                    acc = term if acc is None else acc + term
                s_taps[jb, pl.ds(pl.multiple_of(c * 8, 8), 8), :] = acc
            return carry

        lax.fori_loop(first, last, channel, 0, unroll=16)

    taps_of(0, chans // 2)
    advance(big_sum, 0, first_sum)
    taps_of(chans // 2, chans)
    total = None
    for s in range(8):
        for jb in range(2):
            term = jnp.dot(
                s_taps[jb, pl.ds(s, chans, stride=8), :],
                gather[(2 * s + jb) * LANES : (2 * s + jb + 1) * LANES, :].astype(F32),
                precision=lax.Precision.HIGHEST,
                preferred_element_type=F32,
            )
            total = term if total is None else total + term
    few[0] = total.T[: few.shape[1]]
    sum_copy(few_sum, 0).start()
    make_patches(range(1, bands - 1))
    finish_rows(1)
    start_cols(1)

    @pl.when(lat == top)
    def _():
        for m in range(HALF):
            fold[m] = ext[rows + HALF + m]
            ext[rows + HALF + m] = jnp.zeros(ext.shape[1:], F32)

    make_patches((0, bands - 1))
    advance(few_sum, 0)

    def fold_step(i, carry):
        c0 = pl.multiple_of(i * TC, TC) if not isinstance(i, int) else i * TC
        for m in range(HALF):
            acc = jnp.zeros((TC, chans), F32)
            for n in range(m + 1):
                a = KS - 1 - m + n
                for b in range(KS):
                    v = fold[n, pl.ds(c0 + (OFF - HALF + b), TC), :]
                    acc = acc + v * taps[a, b : b + 1, :].astype(F32)
            folded[m, pl.ds(c0, TC), :] = acc
        return carry

    @pl.when(lat == top)
    def _():
        lax.fori_loop(1, across - 1, fold_step, 0, unroll=2)

    finish_cols(1)
    advance(big_sum, 1)

    @pl.when(lat == top)
    def _():
        for side in (slice(0, OFF), slice(OFF + cols, 2 * OFF + cols)):
            for m in range(HALF):
                fold[m, side, :] = ext[rows + HALF + m, side, :]
                ext[rows + HALF + m, side, :] = jnp.zeros((OFF, chans), F32)

        fold_step(0, 0)
        fold_step(across - 1, 0)

    @pl.when(lat < top)
    def _():
        folded[...] = jnp.zeros_like(folded)

    piece(0, range(bands))
    piece(pieces - 1, range(bands))
    conv(1, 0, chans // 2)
    advance(big_sum, 2)
    advance(few_sum, 1)
    conv(1, chans // 2, chans)
    advance(few_sum, 2)

    def last_step(u, carry):
        at = pl.ds(pl.multiple_of(u * TC, TC), TC)
        for q in range(bands):
            direct = y[pl.ds(u * bands + q, chans, stride=pitch), :].T.reshape(TR, TC, chans)
            total = direct + cot[q * TR : (q + 1) * TR, at, :].astype(F32)
            if q == bands - 1:
                out[q * TR : rows - HALF, at, :] = total[: TR - HALF].astype(BF16)
                out[rows - HALF : rows, at, :] = (total[TR - HALF :] + folded[:, at, :]).astype(BF16)
            else:
                out[q * TR : (q + 1) * TR, at, :] = total.astype(BF16)
        return carry

    parts = grad_sem.shape[0]
    writes = []
    for n in range(parts):
        lax.fori_loop(n * across // parts, (n + 1) * across // parts, last_step, 0)
        at = pl.ds(n * cols // parts, cols // parts)
        writes.append(pltpu.make_async_copy(out.at[:, at], grad.at[:, at], grad_sem.at[n]))
        writes[n].start()
    advance(big_sum, 3)
    advance(few_sum, 3)
    for k in range(4, len(route)):
        advance(big_sum, k)
        advance(few_sum, k)
    totals[: small + 8, :] = big[len(route)]
    totals[small + 8 :, :] = few[len(route)]
    for copy in writes:
        copy.wait()


def results_kernel(
    scale, grad, totals, out, o_in, o_out, o_taps, o_bias, o_gain, o_shift, o_bin, held, come, gone
):
    rows = grad.shape[0]
    in_share, chans = o_in.shape[0], o_out.shape[1]
    small = 2 * in_share + o_out.shape[0]
    parts = come.shape[0]
    depth = rows // parts
    spans = [pl.ds(n * depth, depth) for n in range(parts)]
    reads = [pltpu.make_async_copy(grad.at[at], held.at[at], come.at[n]) for n, at in enumerate(spans)]
    writes = [pltpu.make_async_copy(held.at[at], out.at[at], gone.at[n]) for n, at in enumerate(spans)]
    for copy in reads:
        copy.start()
    for n in range(parts):
        reads[n].wait()
        writes[n].start()
    o_in[:, :chans] = totals[:in_share, :] * scale
    o_in[:, chans:] = totals[in_share : 2 * in_share, :] * scale
    o_out[...] = totals[2 * in_share : small, :] * scale
    for n, ref in enumerate((o_gain, o_shift, o_bias)):
        ref[...] = totals[small + n : small + n + 1, :] * scale
    o_bin[:, :chans] = totals[small + 3 : small + 4, :] * scale
    o_bin[:, chans:] = totals[small + 4 : small + 5, :] * scale
    for a in range(KS):
        o_taps[a] = totals[small + 8 + a * KS : small + 8 + (a + 1) * KS, :] * scale
    for copy in writes:
        copy.wait()


def local(inputs, cotangent, kernel_dw, bias_dw, gain, shift_ln, w_in, b_in, w_out, ocean_mask):
    _, rows, cols, chans = inputs.shape
    hidden = w_in.shape[1]
    hot = spread()
    both = np.zeros((64, 2 * hot.shape[1]), np.float32)
    both[: KS * KS] = np.concatenate([hot, hot[::-1]], 1)
    bands, across = rows // TR, cols // TC
    tiles = bands * across
    steps = len(sum_route())
    shape = jax.ShapeDtypeStruct
    vmem = pl.BlockSpec(memory_space=pltpu.VMEM)
    smem = pl.BlockSpec(memory_space=pltpu.SMEM)
    far = pl.BlockSpec(memory_space=pl.ANY)
    groups = (rows + TR) // 4
    big_rows, few_rows = chans + hidden // 2 + 8, 56
    dma = pltpu.SemaphoreType.DMA
    grad, totals = pl.pallas_call(
        block_kernel,
        out_shape=(shape((rows, cols, chans), BF16), shape((big_rows + few_rows, chans), F32)),
        in_specs=[smem, far, far, far] + [vmem] * 8 + [far],
        out_specs=(far, vmem),
        scratch_shapes=[
            pltpu.VMEM((rows, cols, chans), BF16),
            pltpu.VMEM(both.shape, BF16),
            pltpu.VMEM(gather_taps().shape, BF16),
            pltpu.VMEM((rows + TR, cols + 2 * OFF, chans), F32),
            pltpu.VMEM(((cols // 8 + 1) * chans * (bands + 1), LANES), F32),
            pltpu.VMEM((chans * (tiles + 8), LANES), F32),
            pltpu.VMEM((rows, cols, chans), BF16),
            pltpu.VMEM((chans, 2 * CHUNKS * 16, LANES), BF16),
            pltpu.VMEM((3, chans, LANES), F32),
            pltpu.VMEM((hidden, LANES), F32),
            pltpu.VMEM((2, chans * 8, LANES), F32),
            pltpu.VMEM((chans, hidden), F32),
            pltpu.VMEM((hidden, chans), F32),
            pltpu.VMEM((3 + hidden // chans, chans, LANES), F32),
            pltpu.VMEM((hidden, chans), BF16),
            pltpu.VMEM((2, HALF, cols, chans), BF16),
            pltpu.VMEM((2, 2, HALF, cols, chans), BF16),
            pltpu.VMEM((2, 2, groups, 16, chans), BF16),
            pltpu.VMEM((2, 2, groups, 16, chans), BF16),
            pltpu.VMEM((HALF, cols + 2 * OFF, chans), F32),
            pltpu.VMEM((HALF, cols, chans), F32),
            pltpu.VMEM((steps + 1, big_rows, chans), F32),
            pltpu.VMEM((steps, big_rows, chans), F32),
            pltpu.VMEM((steps + 1, few_rows, chans), F32),
            pltpu.VMEM((steps, few_rows, chans), F32),
            dma((8,)), dma, dma, dma, dma((4,)), dma((2, 5)), dma((2, 5)),
            dma((steps,)), dma((steps,)), dma((steps,)), dma((steps,)),
        ],
        compiler_params=pltpu.CompilerParams(
            collective_id=0, has_side_effects=True, vmem_limit_bytes=63 * 1024 * 1024
        ),
        cost_estimate=pl.CostEstimate(flops=20 << 30, bytes_accessed=12 << 20, transcendentals=4 << 20),
    )(
        ocean_mask, inputs[0], cotangent[0], jnp.asarray(both, BF16), jnp.asarray(row_masks(), BF16), kernel_dw, bias_dw[None],
        gain[None], shift_ln[None], w_in, b_in[None], w_out, jnp.asarray(gather_taps(), BF16),
    )
    cells_all = lax.axis_size("dp") * lax.axis_size("lat") * rows * lax.axis_size("lon") * cols
    grad, s_in, s_out, s_taps, s_bias, s_gain, s_shift, s_bin = pl.pallas_call(
        functools.partial(results_kernel, 1.0 / math.sqrt(cells_all)),
        out_shape=(
            shape((rows, cols, chans), BF16),
            shape((chans // 2, hidden), F32),
            shape((hidden // 2, chans), F32),
            shape((KS, KS, chans), F32),
            shape((1, chans), F32),
            shape((1, chans), F32),
            shape((1, chans), F32),
            shape((1, hidden), F32),
        ),
        in_specs=[far, vmem],
        out_specs=(far,) + (vmem,) * 7,
        scratch_shapes=[pltpu.VMEM((rows, cols, chans), BF16), dma((8,)), dma((8,))],
        compiler_params=pltpu.CompilerParams(vmem_limit_bytes=60 * 1024 * 1024),
    )(grad, totals)
    return grad[None], s_in, s_out, s_taps, s_bias[0], s_gain[0], s_shift[0], s_bin[0]


def solution(mesh):
    field = P(("groups", "dp"), "lat", "lon", None)
    placed = (field, field, P(), P(), P(), P(), P(), P(), P(), P("lat", "lon"))
    return jax.shard_map(
        local,
        mesh=mesh,
        in_specs=placed,
        out_specs=(
            field,
            P(("groups", "dp"), None),
            P(("groups", "dp"), None),
            P("groups", None, None),
            P("groups"),
            P("groups"),
            P("groups"),
            P("groups"),
        ),
        check_vma=False,
    )
```
